32 devices in a mesh: dp: 16 (over z, y, core), tensor: 2 (over x).
Axes of the slice: x: 2, y: 2, z: 4, core: 2. Of those that a mesh axis runs over, the one named last changes fastest.
Arguments:
- tokens: bfloat16 [4096, 768], P(('dp', 'tensor')), may hold values from -6 to 6
- segment_ids: int32 [4096], P('dp'), may hold values from 0 to 31, as said below
- valid_counts: int32 [16], P('dp'), may hold values from 102 to 256, as said below
- ln1_gain: float32 [768], replicated, may hold values from 0.5 to 1.5
- ln1_bias: float32 [768], replicated, may hold values from -3 to 3
- w_qkv: bfloat16 [3, 768, 768], P(None, 'dp', 'tensor'), may hold values from -0.21875 to 0.21875
- b_qv: float32 [2, 768], P(None, 'tensor'), may hold values from -3 to 3
- w_proj: bfloat16 [768, 768], P('dp', 'tensor'), may hold values from -0.625 to 0.625
- b_proj: float32 [768], replicated, may hold values from -3 to 3
- ln2_gain: float32 [768], replicated, may hold values from 0.5 to 1.5
- ln2_bias: float32 [768], replicated, may hold values from -3 to 3
- w_fc: bfloat16 [768, 3072], P('dp', 'tensor'), may hold values from -0.21875 to 0.21875
- b_fc: float32 [3072], P('tensor'), may hold values from -3 to 3
- w_out: bfloat16 [768, 3072], P('dp', 'tensor'), may hold values from -0.109375 to 0.109375
- b_out: float32 [768], replicated, may hold values from -3 to 3
- grad_out: bfloat16 [4096, 768], P(('dp', 'tensor')), may hold values from -6 to 6
Outputs:
- block_out: bfloat16 [4096, 768], P(('dp', 'tensor'))
- grad_input: bfloat16 [4096, 768], P(('dp', 'tensor'))
- d_ln1_gain: float32 [768], replicated
- d_ln1_bias: float32 [768], replicated
- d_w_qkv: float32 [3, 768, 768], P(None, 'dp', 'tensor')
- d_b_qv: float32 [2, 768], P(None, 'tensor')
- d_w_proj: float32 [768, 768], P('dp', 'tensor')
- d_b_proj: float32 [768], replicated
- d_ln2_gain: float32 [768], replicated
- d_ln2_bias: float32 [768], replicated
- d_w_fc: float32 [768, 3072], P('dp', 'tensor')
- d_b_fc: float32 [3072], P('tensor')
- d_w_out: float32 [768, 3072], P('dp', 'tensor')
- d_b_out: float32 [768], replicated
The draws below stay inside these ranges and needn't reach their ends.
Inputs may be any that keep to these rules, and one draw needn't show every extreme that they name: `segment_ids`: within each group of 256 slots the segment numbers start at 0 at the group's first slot and never fall; slots after the group's valid count continue the numbering of the group; some group reaches the largest number. `valid_counts`: at least 102 tokens of each group are in use, the first ones of its slots; some group is full.
All inputs are finite; a program needn't handle non-finite values.
Results may differ from the reference program's by a relative error of at most 0.014.
Values may be sent and summed in bfloat16 or wider, within the bound.
No kernel may reach another device: no remote copies, remote signals or barrier semaphores. Data moves between devices by JAX's collectives and lax.ppermute only.
A program may use at most 128 MiB of HBM per device.

```python
import jax
import jax.numpy as jnp
from jax import lax

D = 768
HEADS = 12
HD = 64
FF = 3072
CAP = 256
SPAN = 160
TOKENS = 4096


def draw_segment_ids(key, part):
    group_total = TOKENS // CAP
    top_number = CAP // 8 - 1
    marks = jax.random.randint(key, (group_total, CAP), 0, SPAN)
    starts = (marks == 0).astype(jnp.int32)
    slot_index = jnp.arange(CAP, dtype=jnp.int32)
    regular = (slot_index % 8 == 0).astype(jnp.int32)
    chosen = jax.random.randint(jax.random.fold_in(key, 11), (), 0, group_total)
    starts = jnp.where((jnp.arange(group_total) == chosen)[:, None], regular[None, :], starts)
    starts = starts.at[:, 0].set(0)
    numbers = jnp.minimum(jnp.cumsum(starts, axis=1), top_number)
    return numbers.astype(jnp.int32).reshape(TOKENS)


def draw_valid_counts(key, part):
    group_total = TOKENS // CAP
    counts = jax.random.randint(key, (group_total,), 2 * CAP // 5, CAP + 1)
    chosen = jax.random.randint(jax.random.fold_in(key, 7), (), 0, group_total)
    return jnp.where(jnp.arange(group_total) == chosen, CAP, counts).astype(jnp.int32)


def levels(stream_key, shape, cuts, least, largest):
    factor_of, own = 1.0, jax.random.fold_in(stream_key, 6)
    for dim, blocks in cuts:
        draws = jnp.exp(jax.random.uniform(jax.random.fold_in(own, dim), (blocks,), jnp.float32, least / len(cuts), largest / len(cuts)))
        factor_of = factor_of * jnp.repeat(draws, shape[dim] // blocks).reshape([-1 if axis == dim else 1 for axis in range(len(shape))])
    return factor_of


def noise(stream_key, dims, deviation, limit, shards=(), held_as=jnp.bfloat16):
    result = deviation * jax.random.normal(stream_key, dims, jnp.float32)
    if shards:
        result = result * levels(stream_key, dims, shards, -0.22, 0.18)
    return jnp.clip(result, -limit, limit).astype(held_as)


def setup_inputs(seed: int = 0) -> dict:
    keys = jax.random.split(jax.random.key(seed), 17)
    tokens = noise(keys[0], (TOKENS, D), 1.0, 6.0, ((0, 32),))
    segment_ids = draw_segment_ids(jax.random.fold_in(keys[16], 71), 0)
    valid_counts = draw_valid_counts(jax.random.fold_in(keys[16], 71), 0)
    ln1_gain = jnp.clip(1.0 + 0.1 * jax.random.normal(keys[3], (D,), jnp.float32), 0.5, 1.5)
    ln1_bias = noise(keys[4], (D,), 0.3, 3.0, (), jnp.float32)
    w_qkv = noise(keys[5], (3, D, D), D ** -0.5, 0.21875, ((1, 16), (2, 2)))
    b_qv = noise(keys[6], (2, D), 0.3, 3.0, ((1, 2),), jnp.float32)
    w_proj = noise(keys[7], (D, D), (D // 8) ** -0.5, 0.625, ((0, 16), (1, 2)))
    b_proj = noise(keys[8], (D,), 0.3, 3.0, (), jnp.float32)
    ln2_gain = jnp.clip(1.0 + 0.1 * jax.random.normal(keys[9], (D,), jnp.float32), 0.5, 1.5)
    ln2_bias = noise(keys[10], (D,), 0.3, 3.0, (), jnp.float32)
    w_fc = noise(keys[11], (D, FF), D ** -0.5, 0.21875, ((0, 16), (1, 2)))
    b_fc = noise(keys[12], (FF,), 0.5, 3.0, ((0, 2),), jnp.float32)
    w_out = noise(keys[13], (D, FF), FF ** -0.5, 0.109375, ((0, 16), (1, 2)))
    b_out = noise(keys[14], (D,), 0.3, 3.0, (), jnp.float32)
    grad_out = noise(keys[15], (TOKENS, D), 1.0, 6.0, ((0, 32),))
    return {"tokens": tokens, "segment_ids": segment_ids, "valid_counts": valid_counts, "ln1_gain": ln1_gain, "ln1_bias": ln1_bias, "w_qkv": w_qkv, "b_qv": b_qv, "w_proj": w_proj, "b_proj": b_proj, "ln2_gain": ln2_gain, "ln2_bias": ln2_bias, "w_fc": w_fc, "b_fc": b_fc, "w_out": w_out, "b_out": b_out, "grad_out": grad_out}


SCALE = 0.125
EPSILON = 1e-05
GELU_C = 0.7978845608028654

def normalize(row_data):
    mean_rows = lax.optimization_barrier(jnp.mean(row_data, axis=-1, keepdims=True))
    centred = row_data - mean_rows
    inv_std = lax.rsqrt(lax.optimization_barrier(jnp.mean(centred * centred, axis=-1, keepdims=True)) + EPSILON)
    return (centred * inv_std, inv_std)

def norm_back(grad_rows, gain_vec, normed, inv_std):
    scaled = grad_rows * gain_vec
    return inv_std * (scaled - lax.optimization_barrier(jnp.mean(scaled, axis=-1, keepdims=True)) - normed * lax.optimization_barrier(jnp.mean(scaled * normed, axis=-1, keepdims=True)))

def gelu_parts(pre_act):
    tanh_arg = GELU_C * (pre_act + 0.044715 * pre_act * pre_act * pre_act)
    tanh_val = jnp.tanh(tanh_arg)
    act_value = 0.5 * pre_act * (1.0 + tanh_val)
    act_slope = 0.5 * (1.0 + tanh_val) + 0.5 * pre_act * (1.0 - tanh_val * tanh_val) * GELU_C * (1.0 + 3.0 * 0.044715 * pre_act * pre_act)
    return (act_value, act_slope)

def matmul(left, right):
    return jnp.dot(left, right, preferred_element_type=jnp.float32)

def group_pass(weights, x_group, seg_group, count_group, dy_group):
    ln1_gain, ln1_bias, w_qkv, b_qv, w_proj, b_proj, ln2_gain, ln2_bias, w_fc, b_fc, w_out, b_out = weights
    positions = jnp.arange(CAP, dtype=jnp.int32)
    live_rows = (positions < count_group).astype(jnp.float32)[:, None]
    allowed = (seg_group[:, None] == seg_group[None, :]) & (positions[None, :] <= positions[:, None])
    x_float = x_group.astype(jnp.float32)
    hat_one, inv_one = normalize(x_float)
    normed_one = (hat_one * ln1_gain + ln1_bias).astype(jnp.bfloat16)
    query_rows = (matmul(normed_one, w_qkv[0]) + b_qv[0]).astype(jnp.bfloat16)
    key_rows = matmul(normed_one, w_qkv[1]).astype(jnp.bfloat16)
    value_rows = (matmul(normed_one, w_qkv[2]) + b_qv[1]).astype(jnp.bfloat16)
    query_heads = query_rows.reshape(CAP, HEADS, HD).astype(jnp.float32)
    key_heads = key_rows.reshape(CAP, HEADS, HD).astype(jnp.float32)
    value_heads = value_rows.reshape(CAP, HEADS, HD).astype(jnp.float32)
    raw_scores = jnp.einsum('qhd,khd->hqk', query_heads, key_heads) * SCALE
    exp_scores = jnp.where(allowed[None], jnp.exp(raw_scores), jnp.float32(0.0))
    totals = lax.optimization_barrier(jnp.sum(exp_scores, axis=-1, keepdims=True))
    log_totals = jnp.log(totals)
    prob_bf = (exp_scores / totals).astype(jnp.bfloat16)
    mixed = jnp.einsum('hqk,khd->qhd', prob_bf.astype(jnp.float32), value_heads).astype(jnp.bfloat16).reshape(CAP, D)
    resid_one = x_float + matmul(mixed, w_proj.T) + b_proj
    hat_two, inv_two = normalize(resid_one)
    normed_two = (hat_two * ln2_gain + ln2_bias).astype(jnp.bfloat16)
    pre_act = matmul(normed_two, w_fc) + b_fc
    act_value, act_slope = gelu_parts(pre_act)
    act_bf = act_value.astype(jnp.bfloat16)
    block_out = ((resid_one + matmul(act_bf, w_out.T) + b_out) * live_rows).astype(jnp.bfloat16)
    grad_rows = dy_group.astype(jnp.float32) * live_rows
    grad_bf = grad_rows.astype(jnp.bfloat16)
    grad_pre = matmul(grad_bf, w_out) * act_slope
    grad_pre_bf = grad_pre.astype(jnp.bfloat16)
    grad_h2 = matmul(grad_pre_bf, w_fc.T)
    grad_resid = grad_rows + norm_back(grad_h2, ln2_gain, hat_two, inv_two)
    resid_bf = grad_resid.astype(jnp.bfloat16)
    grad_mixed = matmul(resid_bf, w_proj).astype(jnp.bfloat16).reshape(CAP, HEADS, HD).astype(jnp.float32)
    prob_f = jnp.where(allowed[None], jnp.exp(raw_scores - log_totals), jnp.float32(0.0))
    prob_again = prob_f.astype(jnp.bfloat16).astype(jnp.float32)
    grad_prob = jnp.einsum('qhd,khd->hqk', grad_mixed, value_heads)
    delta_rows = lax.optimization_barrier(jnp.sum(prob_f * grad_prob, axis=-1, keepdims=True))
    grad_scores = (prob_f * (grad_prob - delta_rows) * SCALE).astype(jnp.bfloat16).astype(jnp.float32)
    grad_query = jnp.einsum('hqk,khd->qhd', grad_scores, key_heads).reshape(CAP, D)
    grad_key = jnp.einsum('hqk,qhd->khd', grad_scores, query_heads).reshape(CAP, D)
    grad_value = jnp.einsum('hqk,qhd->khd', prob_again, grad_mixed).reshape(CAP, D)
    query_grad_bf = grad_query.astype(jnp.bfloat16)
    key_grad_bf = grad_key.astype(jnp.bfloat16)
    value_grad_bf = grad_value.astype(jnp.bfloat16)
    grad_h1 = matmul(query_grad_bf, w_qkv[0].T) + matmul(key_grad_bf, w_qkv[1].T) + matmul(value_grad_bf, w_qkv[2].T)
    grad_input = (grad_resid + norm_back(grad_h1, ln1_gain, hat_one, inv_one)).astype(jnp.bfloat16)
    grads = (lax.optimization_barrier(jnp.sum(grad_h1 * hat_one, axis=0)), lax.optimization_barrier(jnp.sum(grad_h1, axis=0)), jnp.stack([matmul(normed_one.T, query_grad_bf), matmul(normed_one.T, key_grad_bf), matmul(normed_one.T, value_grad_bf)]), jnp.stack([lax.optimization_barrier(jnp.sum(grad_query, axis=0)), lax.optimization_barrier(jnp.sum(grad_value, axis=0))]), matmul(resid_bf.T, mixed), lax.optimization_barrier(jnp.sum(grad_resid, axis=0)), lax.optimization_barrier(jnp.sum(grad_h2 * hat_two, axis=0)), lax.optimization_barrier(jnp.sum(grad_h2, axis=0)), matmul(normed_two.T, grad_pre_bf), lax.optimization_barrier(jnp.sum(grad_pre, axis=0)), matmul(grad_bf.T, act_bf), lax.optimization_barrier(jnp.sum(grad_rows, axis=0)))
    return (block_out, grad_input, grads)

def reference(tokens, segment_ids, valid_counts, ln1_gain, ln1_bias, w_qkv, b_qv, w_proj, b_proj, ln2_gain, ln2_bias, w_fc, b_fc, w_out, b_out, grad_out):
    group_total = TOKENS // CAP
    weights = (ln1_gain, ln1_bias, w_qkv, b_qv, w_proj, b_proj, ln2_gain, ln2_bias, w_fc, b_fc, w_out, b_out)
    inputs = (tokens.reshape(group_total, CAP, D), segment_ids.reshape(group_total, CAP), valid_counts, grad_out.reshape(group_total, CAP, D))
    zero_grads = (jnp.zeros((D,), jnp.float32), jnp.zeros((D,), jnp.float32), jnp.zeros((3, D, D), jnp.float32), jnp.zeros((2, D), jnp.float32), jnp.zeros((D, D), jnp.float32), jnp.zeros((D,), jnp.float32), jnp.zeros((D,), jnp.float32), jnp.zeros((D,), jnp.float32), jnp.zeros((D, FF), jnp.float32), jnp.zeros((FF,), jnp.float32), jnp.zeros((D, FF), jnp.float32), jnp.zeros((D,), jnp.float32))

    def scan_step(carry, item):
        out_rows, input_rows, grads = group_pass(weights, item[0], item[1], item[2], item[3])
        return (tuple((left + right for left, right in zip(carry, grads))), (out_rows, input_rows))
    totals, (out_all, input_all) = lax.scan(scan_step, zero_grads, inputs)
    return (out_all.reshape(TOKENS, D), input_all.reshape(TOKENS, D), totals[0], totals[1], totals[2], totals[3], totals[4], totals[5], totals[6], totals[7], totals[8], totals[9], totals[10], totals[11])
```

```python
import functools

import jax
import jax.numpy as jnp
from jax import lax
from jax.experimental import pallas as pl
from jax.experimental.pallas import tpu as pltpu
from jax.sharding import PartitionSpec as P

HD = 64


SCALE = 0.125
EPSILON = 1e-05
GELU_C = 0.7978845608028654


def normalize(row_data):
    mean_rows = jnp.mean(row_data, axis=-1, keepdims=True)
    centred = row_data - mean_rows
    inv_std = lax.rsqrt(jnp.mean(centred * centred, axis=-1, keepdims=True) + EPSILON)
    return (centred * inv_std, inv_std)


def norm_back(grad_rows, gain_vec, normed, inv_std):
    scaled = grad_rows * gain_vec
    return inv_std * (
        scaled
        - jnp.mean(scaled, axis=-1, keepdims=True)
        - normed * jnp.mean(scaled * normed, axis=-1, keepdims=True)
    )


def gelu_parts(pre_act):
    tanh_arg = GELU_C * (pre_act + 0.044715 * pre_act * pre_act * pre_act)
    tanh_val = jnp.tanh(tanh_arg)
    act_value = 0.5 * pre_act * (1.0 + tanh_val)
    act_slope = 0.5 * (1.0 + tanh_val) + 0.5 * pre_act * (1.0 - tanh_val * tanh_val) * GELU_C * (
        1.0 + 3.0 * 0.044715 * pre_act * pre_act
    )
    return (act_value, act_slope)


def matmul(left, right):
    return jnp.dot(left, right, preferred_element_type=jnp.float32)


def matmul_nt(left, right):
    return lax.dot_general(
        left, right, (((1,), (1,)), ((), ())), preferred_element_type=jnp.float32
    )


def matmul_tn(left, right):
    return lax.dot_general(
        left, right, (((0,), (0,)), ((), ())), preferred_element_type=jnp.float32
    )


def bf(value):
    return value.astype(jnp.bfloat16)


def core_swap(value):
    count = lax.axis_size("dp")
    return lax.ppermute(value, "dp", [(i, i ^ 1) for i in range(count)])


def x_swap(value):
    return lax.ppermute(value, "tensor", [(0, 1), (1, 0)])


def use_ring(shard_rows):
    return lax.axis_size("dp") <= 16 and shard_rows % 16 == 0


def ring_chips(chip_count):
    return list(range(0, chip_count, 2)) + list(range(1, chip_count, 2))[::-1]


def ring_send(value, step):
    chips = ring_chips(lax.axis_size("dp") // 2)
    size = len(chips)
    pairs = []
    for place, chip in enumerate(chips):
        other = chips[(place + step) % size]
        pairs += [(2 * chip, 2 * other), (2 * chip + 1, 2 * other + 1)]
    return lax.ppermute(value, "dp", pairs)


def ring_place(chip, size):
    return jnp.where(chip % 2 == 0, chip // 2, size - 1 - chip // 2)


def ring_chip(place, size):
    place = place % size
    return jnp.where(place < size // 2, 2 * place, 2 * (size - 1 - place) + 1)


def assemble_kernel(index_ref, *refs):
    count = index_ref.shape[0]
    pieces, out_ref, sems = refs[:-2], refs[-2], refs[-1]
    rows = out_ref.shape[0] // count
    copies = []
    for piece in pieces:
        for part in range(piece.shape[0] // rows):
            slot = len(copies)
            start = pl.multiple_of(index_ref[slot] * rows, rows)
            copy = pltpu.make_async_copy(
                piece.at[pl.ds(part * rows, rows)], out_ref.at[pl.ds(start, rows)], sems.at[slot]
            )
            copy.start()
            copies.append(copy)
    for copy in copies:
        copy.wait()


def assemble(index, pieces, rows, columns):
    count = index.shape[0]
    return pl.pallas_call(
        assemble_kernel,
        out_shape=jax.ShapeDtypeStruct((rows, columns), jnp.bfloat16),
        grid_spec=pltpu.PrefetchScalarGridSpec(
            num_scalar_prefetch=1,
            grid=(1,),
            in_specs=[pl.BlockSpec(memory_space=pl.ANY)] * len(pieces),
            out_specs=pl.BlockSpec((rows, columns), lambda i, index: (0, 0)),
            scratch_shapes=[pltpu.SemaphoreType.DMA((count,))],
        ),
        compiler_params=pltpu.CompilerParams(vmem_limit_bytes=8 << 20),
    )(index, *pieces)


def gather_rows(chip_block):
    device_count = lax.axis_size("dp")
    me = lax.axis_index("dp")
    size = device_count // 2
    core, place = me % 2, ring_place(me // 2, size)
    half = chip_block.shape[0] // 2
    pieces, index = [chip_block], []

    def owners(offset):
        chip = ring_chip(place + offset, size)
        return [2 * chip + core, 2 * chip + 1 - core]

    index += owners(0)
    ahead = back = chip_block
    for step in range(1, size // 2):
        ahead, back = ring_send(ahead, 1), ring_send(back, -1)
        pieces += [ahead, back]
        index += owners(-step) + owners(step)
    pieces += [ring_send(ahead[:half], 1), ring_send(back[half:], -1)]
    index += owners(size // 2)
    return pieces, jnp.stack(index).astype(jnp.int32)


def reduce_rows(block_of, half):
    size = lax.axis_size("dp") // 2
    far = block_of(size // 2)
    ahead = ring_send(bf(far[:half]), 1)
    back = ring_send(bf(far[half:]), -1)
    for step in range(size // 2 - 1, 0, -1):
        up, down = block_of(step).astype(jnp.float32), block_of(-step).astype(jnp.float32)
        if ahead.shape[0] == half:
            up = jnp.concatenate([up[:half] + ahead.astype(jnp.float32), up[half:]], axis=0)
            down = jnp.concatenate([down[:half], down[half:] + back.astype(jnp.float32)], axis=0)
        else:
            up = up + ahead.astype(jnp.float32)
            down = down + back.astype(jnp.float32)
        ahead, back = ring_send(bf(up), 1), ring_send(bf(down), -1)
    return block_of(0).astype(jnp.float32) + ahead.astype(jnp.float32) + back.astype(jnp.float32)


def reduce_weight(full):
    device_count = lax.axis_size("dp")
    me = lax.axis_index("dp")
    size = device_count // 2
    core, place = me % 2, ring_place(me // 2, size)
    rows = full.shape[0] // size
    half = rows // 2
    if not use_ring(half):
        none = jnp.zeros_like(full)
        wide = jnp.concatenate(
            [jnp.where(core == 0, full, none), jnp.where(core == 0, none, full)], axis=1
        )
        parts = lax.all_to_all(wide, "dp", split_axis=0, concat_axis=0, tiled=True)
        total = jnp.sum(parts.astype(jnp.float32).reshape(device_count, half, -1), axis=0)
        return total[:, : full.shape[1]], total[:, full.shape[1] :]

    def block_of(offset):
        chip = ring_chip(place + offset, size)
        return lax.dynamic_slice_in_dim(full, chip * rows, rows, axis=0)

    total = reduce_rows(block_of, half)
    own = lax.dynamic_slice_in_dim(total, core * half, half, axis=0)
    other = core_swap(lax.dynamic_slice_in_dim(total, (1 - core) * half, half, axis=0))
    return jnp.where(core == 0, own, other), jnp.where(core == 0, other, own)


def core_part(array, core, axis):
    width = array.shape[axis] // 2
    return lax.dynamic_slice_in_dim(array, core * width, width, axis=axis)


def swap_halves(rows):
    half = rows.shape[0] // 2
    return jnp.concatenate([rows[half:], rows[:half]], axis=0)


def swap_pairs(rows):
    half = rows.shape[0] // 2
    return jnp.concatenate([swap_halves(rows[:half]), swap_halves(rows[half:])], axis=0)


def rows_to_owners(partial):
    half = partial.shape[0] // 2
    quarter = half // 2
    pair = partial[:half] + core_swap(bf(partial[half:])).astype(jnp.float32)
    return pair[:quarter] + x_swap(bf(pair[quarter:])).astype(jnp.float32)


def local(
    tokens,
    segment_ids,
    valid_counts,
    ln1_gain,
    ln1_bias,
    w_qkv,
    b_qv,
    w_proj,
    b_proj,
    ln2_gain,
    ln2_bias,
    w_fc,
    b_fc,
    w_out,
    b_out,
    grad_out,
):
    me, side = lax.axis_index("dp"), lax.axis_index("tensor")
    core = me % 2
    row_count, width = tokens.shape
    group_rows = 2 * row_count
    all_rows = 2 * group_rows
    shard_rows = w_fc.shape[0]
    positions = side * row_count + jnp.arange(row_count, dtype=jnp.int32)
    live_rows = (positions < valid_counts[0]).astype(jnp.float32)[:, None]
    grad_own = bf(grad_out.astype(jnp.float32) * live_rows)

    quarter = w_qkv.shape[2] // 2

    def pack_one(which):
        q = core_part(w_qkv, which, 2)
        return jnp.concatenate([q[0], q[1], q[2], core_part(w_proj, which, 1)], axis=1)

    def chip_rows(kept, sent):
        return jnp.concatenate([kept, core_swap(sent)], axis=0)

    if use_ring(shard_rows):
        chip_one = chip_rows(pack_one(core), pack_one(1 - core))
        chip_fc = chip_rows(core_part(w_fc, core, 1), core_part(w_fc, 1 - core, 1))
        chip_out = chip_rows(core_part(w_out, core, 1), core_part(w_out, 1 - core, 1))
        one_pieces, index = gather_rows(chip_one)
        fc_pieces, _ = gather_rows(chip_fc)
        out_pieces, _ = gather_rows(chip_out)
        one_full = assemble(index, one_pieces, width, chip_one.shape[1])
        fc_full = assemble(index, fc_pieces, width, chip_fc.shape[1])
        out_full = assemble(index, out_pieces, width, chip_out.shape[1])
    else:
        both_one = jnp.concatenate([pack_one(0), pack_one(1)], axis=1)
        one_full, fc_full, out_full = (
            core_part(lax.all_gather(shard, "dp", axis=0, tiled=True), core, 1)
            for shard in (both_one, w_fc, w_out)
        )

    own_pair = jnp.stack([tokens, grad_own])
    x_pair = x_swap(own_pair)
    core_pair = core_swap(own_pair)
    far_pair = core_swap(x_pair)
    x_all = jnp.concatenate([own_pair[0], x_pair[0], core_pair[0], far_pair[0]], axis=0)
    grad_all = jnp.concatenate([own_pair[1], x_pair[1], core_pair[1], far_pair[1]], axis=0)
    seg_own = jnp.where(side == 0, segment_ids, swap_halves(segment_ids))
    segs = jnp.stack([seg_own, core_swap(seg_own)])
    slots = jnp.concatenate([positions, (1 - side) * row_count + jnp.arange(row_count, dtype=jnp.int32)])
    allowed = (segs[:, :, None] == segs[:, None, :]) & (slots[None, :] <= slots[:, None])[None]

    x_float = x_all.astype(jnp.float32)
    hat_one, inv_one = normalize(x_float)
    normed_one = bf(hat_one * ln1_gain + ln1_bias)
    bias_qv = core_part(b_qv, core, 1)
    query = bf(matmul(normed_one, one_full[:, :quarter]) + bias_qv[0])
    keys = bf(matmul(normed_one, one_full[:, quarter : 2 * quarter]))
    values = bf(matmul(normed_one, one_full[:, 2 * quarter : 3 * quarter]) + bias_qv[1])
    proj_own = one_full[:, 3 * quarter :]

    def heads(rows):
        return rows.reshape(2, group_rows, quarter // HD, HD)

    query_h, key_h, value_h = heads(query), heads(keys), heads(values)
    scores = jnp.einsum("gqhd,gkhd->ghqk", query_h, key_h, preferred_element_type=jnp.float32) * SCALE
    exp_scores = jnp.where(allowed[:, None], jnp.exp(scores), 0.0)
    totals = jnp.sum(exp_scores, axis=-1, keepdims=True)
    prob_f = exp_scores / totals
    prob_bf = bf(prob_f)
    mixed = bf(
        jnp.einsum("ghqk,gkhd->gqhd", prob_bf, value_h, preferred_element_type=jnp.float32)
    ).reshape(all_rows, quarter)
    mixed_x, proj_x = x_swap(mixed), x_swap(proj_own)
    mixed_c, mixed_cx = core_swap(mixed), core_swap(mixed_x)
    proj_c, proj_cx = core_swap(proj_own), core_swap(proj_x)
    mixed_all = jnp.concatenate(
        [mixed, swap_pairs(mixed_x), swap_halves(mixed_c), swap_halves(swap_pairs(mixed_cx))], axis=1
    )
    proj_all = jnp.concatenate([proj_own, proj_x, proj_c, proj_cx], axis=1)
    resid_one = x_float + matmul_nt(mixed_all, proj_all) + b_proj
    hat_two, inv_two = normalize(resid_one)
    normed_two = bf(hat_two * ln2_gain + ln2_bias)
    pre_act = matmul(normed_two, fc_full) + core_part(b_fc, core, 0)
    act_value, act_slope = gelu_parts(pre_act)
    act_bf = bf(act_value)
    d_out_terms = bf(matmul_tn(grad_all, act_bf))
    d_out = reduce_weight(d_out_terms)

    grad_pre = matmul(grad_all, out_full) * act_slope
    grad_pre_bf = bf(grad_pre)
    h2_part = matmul_nt(grad_pre_bf, fc_full)
    h2_pair = h2_part[:group_rows] + core_swap(bf(h2_part[group_rows:])).astype(jnp.float32)
    h2_own = h2_pair + swap_halves(x_swap(bf(h2_pair))).astype(jnp.float32)
    h2_other = core_swap(bf(h2_own)).astype(jnp.float32)
    d_fc_terms = bf(matmul_tn(normed_two, grad_pre_bf))
    d_fc = reduce_weight(d_fc_terms)
    mlp_rows = rows_to_owners(matmul_nt(act_bf, out_full))
    block_out = bf((resid_one[:row_count] + mlp_rows + b_out) * live_rows)

    grad_h2 = jnp.concatenate([h2_own, h2_other], axis=0)
    grad_resid = grad_all.astype(jnp.float32) + norm_back(grad_h2, ln2_gain, hat_two, inv_two)
    resid_bf = bf(grad_resid)
    grad_mixed = heads(bf(matmul(resid_bf, proj_own)))
    prob_again = prob_bf
    grad_prob = jnp.einsum("gqhd,gkhd->ghqk", grad_mixed, value_h, preferred_element_type=jnp.float32)
    delta = jnp.sum(prob_f * grad_prob, axis=-1, keepdims=True)
    grad_scores = bf(prob_f * (grad_prob - delta) * SCALE)
    grad_query = jnp.einsum(
        "ghqk,gkhd->gqhd", grad_scores, key_h, preferred_element_type=jnp.float32
    ).reshape(all_rows, quarter)
    grad_key = jnp.einsum(
        "ghqk,gqhd->gkhd", grad_scores, query_h, preferred_element_type=jnp.float32
    ).reshape(all_rows, quarter)
    grad_value = jnp.einsum(
        "ghqk,gqhd->gkhd", prob_again, grad_mixed, preferred_element_type=jnp.float32
    ).reshape(all_rows, quarter)
    joined = jnp.concatenate([bf(grad_query), bf(grad_key), bf(grad_value)], axis=1)
    d_one_terms = jnp.concatenate(
        [bf(matmul_tn(normed_one, joined)), bf(matmul_tn(resid_bf, mixed))], axis=1
    )
    d_one = reduce_weight(d_one_terms)
    h1_part = matmul_nt(joined, one_full[:, : 3 * quarter])
    grad_h1 = rows_to_owners(h1_part)
    grad_input = bf(
        grad_resid[:row_count] + norm_back(grad_h1, ln1_gain, hat_one[:row_count], inv_one[:row_count])
    )

    pad = jnp.zeros((width - 2 * quarter,), jnp.float32)
    sums = jnp.stack(
        [
            jnp.sum(h1_part * hat_one, axis=0),
            jnp.sum(h1_part, axis=0),
            jnp.sum(grad_h2[:row_count] * hat_two[:row_count], axis=0),
            jnp.sum(grad_h2[:row_count], axis=0),
            jnp.sum(grad_resid[:row_count], axis=0),
            jnp.sum(grad_own.astype(jnp.float32), axis=0),
        ]
    )
    bias_sums = jnp.stack(
        [
            jnp.sum(grad_pre, axis=0),
            jnp.concatenate([jnp.sum(grad_query, axis=0), jnp.sum(grad_value, axis=0), pad]),
        ]
    )
    both = jnp.concatenate([sums, bias_sums], axis=0)
    met = core_swap(both)
    sums = sums + met[:6]
    sums = sums + x_swap(sums)
    both = jnp.concatenate([sums, bias_sums, met[6:]], axis=0)
    reach = 2
    while reach < lax.axis_size("dp"):
        both = both + lax.ppermute(
            both, "dp", [(i, i ^ reach) for i in range(lax.axis_size("dp"))]
        )
        reach *= 2
    sums = both[:6]
    low = jnp.where(core == 0, both[6:8], both[8:10])
    high = jnp.where(core == 0, both[8:10], both[6:8])
    d_bfc = jnp.concatenate([low[0], high[0]])
    d_qv = jnp.concatenate(
        [low[1, : 2 * quarter].reshape(2, quarter), high[1, : 2 * quarter].reshape(2, quarter)], axis=1
    )
    parts = [half.reshape(shard_rows, 4, quarter) for half in d_one]
    d_four = jnp.concatenate(parts, axis=2).transpose(1, 0, 2)
    return (
        block_out,
        grad_input,
        sums[0],
        sums[1],
        d_four[:3],
        d_qv,
        d_four[3],
        sums[4],
        sums[2],
        sums[3],
        jnp.concatenate(d_fc, axis=1),
        d_bfc,
        jnp.concatenate(d_out, axis=1),
        sums[5],
    )


def solution(mesh):
    return jax.shard_map(
        local,
        mesh=mesh,
        in_specs=(
            P(("dp", "tensor"), None),
            P("dp"),
            P("dp"),
            P(),
            P(),
            P(None, "dp", "tensor"),
            P(None, "tensor"),
            P("dp", "tensor"),
            P(),
            P(),
            P(),
            P("dp", "tensor"),
            P("tensor"),
            P("dp", "tensor"),
            P(),
            P(("dp", "tensor"), None),
        ),
        out_specs=(
            P(("dp", "tensor"), None),
            P(("dp", "tensor"), None),
            P(),
            P(),
            P(None, "dp", "tensor"),
            P(None, "tensor"),
            P("dp", "tensor"),
            P(),
            P(),
            P(),
            P("dp", "tensor"),
            P("tensor"),
            P("dp", "tensor"),
            P(),
        ),
        check_vma=False,
    )
```

```python
import functools

import jax
import jax.numpy as jnp
from jax import lax
from jax.experimental import pallas as pl
from jax.experimental.pallas import tpu as pltpu
from jax.sharding import PartitionSpec as P


HD = 64


SCALE = 0.125
EPSILON = 1e-05
GELU_C = 0.7978845608028654

VMEM_LIMIT = 20 << 20
VMEM = pl.BlockSpec(memory_space=pltpu.VMEM)
SMEM = pl.BlockSpec(memory_space=pltpu.SMEM)
HBM = pl.BlockSpec(memory_space=pltpu.HBM)


def normalize(row_data):
    mean_rows = jnp.mean(row_data, axis=-1, keepdims=True)
    centred = row_data - mean_rows
    inv_std = lax.rsqrt(jnp.mean(centred * centred, axis=-1, keepdims=True) + EPSILON)
    return (centred * inv_std, inv_std)


def norm_back(grad_rows, gain_vec, normed, inv_std):
    scaled = grad_rows * gain_vec
    return inv_std * (
        scaled
        - jnp.mean(scaled, axis=-1, keepdims=True)
        - normed * jnp.mean(scaled * normed, axis=-1, keepdims=True)
    )


def gelu_parts(pre_act):
    tanh_arg = GELU_C * (pre_act + 0.044715 * pre_act * pre_act * pre_act)
    tanh_val = jnp.tanh(tanh_arg)
    act_value = 0.5 * pre_act * (1.0 + tanh_val)
    act_slope = 0.5 * (1.0 + tanh_val) + 0.5 * pre_act * (1.0 - tanh_val * tanh_val) * GELU_C * (
        1.0 + 3.0 * 0.044715 * pre_act * pre_act
    )
    return (act_value, act_slope)


def bf(value):
    return value.astype(jnp.bfloat16)


def core_swap(value):
    count = lax.axis_size("dp")
    return lax.ppermute(value, "dp", [(i, i ^ 1) for i in range(count)])


def x_swap(value):
    return lax.ppermute(value, "tensor", [(0, 1), (1, 0)])


def use_ring(shard_rows):
    return lax.axis_size("dp") <= 16 and shard_rows % 16 == 0


def ring_chips(chip_count):
    return list(range(0, chip_count, 2)) + list(range(1, chip_count, 2))[::-1]


def ring_send(value, step):
    chips = ring_chips(lax.axis_size("dp") // 2)
    size = len(chips)
    pairs = []
    for place, chip in enumerate(chips):
        other = chips[(place + step) % size]
        pairs += [(2 * chip, 2 * other), (2 * chip + 1, 2 * other + 1)]
    return lax.ppermute(value, "dp", pairs)


CORE, SIDE, CHIP, FAR, STEPS = 0, 1, 2, 3, 4


def table_size(chips):
    return 4 + 2 * (chips // 2) + 2 * chips


def fill_table(table_ref, chips):
    def chip_at(place):
        place = lax.rem(place + chips, chips)
        return jnp.where(place < chips // 2, 2 * place, 2 * (chips - 1 - place) + 1)

    me = lax.axis_index("dp")
    core, chip = lax.rem(me, 2), lax.div(me, 2)
    place = jnp.where(lax.rem(chip, 2) == 0, lax.div(chip, 2), chips - 1 - lax.div(chip, 2))
    table_ref[CORE] = core
    table_ref[SIDE] = lax.axis_index("tensor")
    table_ref[CHIP] = chip
    table_ref[FAR] = chip_at(place + chips // 2)
    entry = STEPS
    for step in range(1, chips // 2 + 1):
        table_ref[entry] = chip_at(place + step)
        table_ref[entry + 1] = chip_at(place - step)
        entry += 2
    offsets = [0]
    for step in range(1, chips // 2):
        offsets += [-step, step]
    for offset in offsets + [chips // 2]:
        owner = chip_at(place + offset)
        table_ref[entry] = 2 * owner + core
        table_ref[entry + 1] = 2 * owner + 1 - core
        entry += 2


def fill(index_ref, pieces, outs, sems):
    count = sems.shape[0] // len(outs)
    base = index_ref.shape[0] - count
    rows = outs[0].shape[0] // count
    copies = []
    slot = 0
    for piece in pieces:
        for part in range(piece.shape[0] // rows):
            start = pl.multiple_of(index_ref[base + slot] * rows, rows)
            column = 0
            for out in outs:
                source = piece.at[pl.ds(part * rows, rows), pl.ds(column, out.shape[1])]
                copy = pltpu.make_async_copy(source, out.at[pl.ds(start, rows)], sems.at[len(copies)])
                copy.start()
                copies.append(copy)
                column += out.shape[1]
            slot += 1
    return copies


def assemble_one_kernel(index_ref, *refs):
    pieces, out_ref, proj_ref, sems = refs[:-3], refs[-3], refs[-2], refs[-1]
    for copy in fill(index_ref, pieces, (out_ref,), sems):
        copy.wait()
    quarter = proj_ref.shape[0]
    for block in range(4):
        here = slice(block * quarter, (block + 1) * quarter)
        proj_ref[:, here] = out_ref[here, 3 * quarter :]


def assemble_one(index, pieces, width, count):
    quarter = width // 4
    outs = (
        jax.ShapeDtypeStruct((width, width), jnp.bfloat16),
        jax.ShapeDtypeStruct((quarter, width), jnp.bfloat16),
    )
    return pl.pallas_call(
        assemble_one_kernel,
        out_shape=outs,
        in_specs=[SMEM] + [pl.BlockSpec(memory_space=pl.ANY)] * len(pieces),
        out_specs=[VMEM] * len(outs),
            scratch_shapes=[pltpu.SemaphoreType.DMA((count,))],
        compiler_params=pltpu.CompilerParams(vmem_limit_bytes=VMEM_LIMIT),
        cost_estimate=pl.CostEstimate(flops=0, bytes_accessed=3 << 20, transcendentals=0),
    )(index, *pieces)


def gather_rows(chip_block):
    size = lax.axis_size("dp") // 2
    half = chip_block.shape[0] // 2
    pieces = [chip_block]
    ahead = back = chip_block
    for _ in range(1, size // 2):
        ahead = ring_send(ahead, 1)
        back = ring_send(back, -1)
        pieces += [ahead, back]
    pieces.append(ring_send(ahead[:half], 1))
    pieces.append(ring_send(back[half:], -1))
    return pieces


def send_far(table_ref, full_ref, ahead_ref, back_ref):
    cut = ahead_ref.shape[0]
    rows = cut + back_ref.shape[0]
    block = full_ref[pl.ds(pl.multiple_of(table_ref[FAR] * rows, 16), rows), :]
    ahead_ref[...] = block[:cut]
    back_ref[...] = block[cut:]


def step_kernel(table_ref, full_ref, ahead_ref, back_ref, up_ref, down_ref, *, step):
    rows = up_ref.shape[0]
    head, tail = ahead_ref.shape[0], back_ref.shape[0]
    at_up, at_down = table_ref[STEPS + 2 * (step - 1)], table_ref[STEPS + 2 * (step - 1) + 1]
    up = full_ref[pl.ds(pl.multiple_of(at_up * rows, 16), rows), :]
    down = full_ref[pl.ds(pl.multiple_of(at_down * rows, 16), rows), :]
    up_ref[...] = up
    down_ref[...] = down
    up_ref[:head, :] = bf(up[:head].astype(jnp.float32) + ahead_ref[...].astype(jnp.float32))
    down_ref[rows - tail :, :] = bf(
        down[rows - tail :].astype(jnp.float32) + back_ref[...].astype(jnp.float32)
    )


def last_kernel(table_ref, full_ref, ahead_ref, back_ref, keep_ref, send_ref):
    rows = ahead_ref.shape[0]
    kept = keep_ref.shape[0]
    half = rows - kept
    block = full_ref[pl.ds(pl.multiple_of(table_ref[CHIP] * rows, 16), rows), :]
    total = block.astype(jnp.float32) + ahead_ref[...].astype(jnp.float32)
    total = total + back_ref[...].astype(jnp.float32)
    for core in range(2):

        @pl.when(table_ref[CORE] == core)
        def _():
            for ref, part in ((keep_ref, core), (send_ref, 1 - core)):
                ref[:half, :] = total[:half] if part == 0 else total[kept:]
                if kept > half:
                    ref[half:, :] = total[half:kept]


def ring_call(kernel, outs, *ins):
    return pl.pallas_call(
        kernel,
        out_shape=outs,
        in_specs=[SMEM] + [VMEM] * (len(ins) - 1),
        out_specs=[VMEM] * len(outs),
        compiler_params=pltpu.CompilerParams(vmem_limit_bytes=8 << 20),
        cost_estimate=pl.CostEstimate(flops=0, bytes_accessed=1 << 20, transcendentals=0),
    )(*ins)


def reduce_ring(table, full, far, half):
    size = lax.axis_size("dp") // 2
    rows, columns = full.shape[0] // size, full.shape[1]
    ahead = ring_send(far[0], 1)
    back = ring_send(far[1], -1)
    message = jax.ShapeDtypeStruct((rows, columns), jnp.bfloat16)
    for step in range(size // 2 - 1, 0, -1):
        kernel = functools.partial(step_kernel, step=step)
        up, down = ring_call(kernel, (message, message), table, full, ahead, back)
        ahead = ring_send(up, 1)
        back = ring_send(down, -1)
    kept = jax.ShapeDtypeStruct((rows - half, columns), jnp.float32)
    keep, send = ring_call(last_kernel, (kept, kept), table, full, ahead, back)
    return keep, core_swap(send)


def reduce_plain(full):
    device_count = lax.axis_size("dp")
    core = lax.axis_index("dp") % 2
    none = jnp.zeros_like(full)
    wide = jnp.concatenate(
        [jnp.where(core == 0, full, none), jnp.where(core == 0, none, full)], axis=1
    )
    parts = lax.all_to_all(wide, "dp", split_axis=0, concat_axis=0, tiled=True)
    rows = full.shape[0] // device_count
    total = jnp.sum(parts.astype(jnp.float32).reshape(device_count, rows, -1), axis=0)
    left, right = total[:, : full.shape[1]], total[:, full.shape[1] :]
    return jnp.where(core == 0, left, right), jnp.where(core == 0, right, left)


def pack_kernel(
    qkv_hbm, proj_hbm, fc_hbm, out_hbm, keep_one, send_one, keep_two, send_two, qkv_ref, proj_ref, sems
):
    quarter = proj_ref.shape[1] // 2
    hidden = fc_hbm.shape[1] // 2
    me_core = lax.rem(lax.axis_index("dp"), 2)
    copies = [
        pltpu.make_async_copy(qkv_hbm, qkv_ref, sems.at[0]),
        pltpu.make_async_copy(proj_hbm, proj_ref, sems.at[1]),
    ]
    for place, (two, part) in enumerate(((keep_two, me_core), (send_two, 1 - me_core))):
        for half, source in enumerate((fc_hbm, out_hbm)):
            at = pl.ds(pl.multiple_of(part * hidden, 128), hidden)
            into = two.at[:, pl.ds(half * hidden, hidden)]
            copies.append(pltpu.make_async_copy(source.at[:, at], into, sems.at[2 + 2 * place + half]))
    for copy in copies:
        copy.start()
    copies[0].wait()
    copies[1].wait()
    for core in range(2):

        @pl.when(me_core == core)
        def _():
            for one, part in ((keep_one, core), (send_one, 1 - core)):
                at = slice(part * quarter, (part + 1) * quarter)
                for which in range(3):
                    one[:, which * quarter : (which + 1) * quarter] = qkv_ref[which, :, at]
                one[:, 3 * quarter :] = proj_ref[:, at]

    for copy in copies[2:]:
        copy.wait()


def fill_params(me_core, vectors, params_ref, quarter):
    width = params_ref.shape[1]
    g1_ref, b1_ref, bqv_ref, bp_ref, g2_ref, b2_ref, bfc_ref, bo_ref = vectors
    for place, ref in ((0, g1_ref), (1, b1_ref), (3, bp_ref), (4, g2_ref), (5, b2_ref), (7, bo_ref)):
        params_ref[place : place + 1, :] = ref[...].reshape(1, width)
    params_ref[2:3, :] = jnp.zeros((1, width), jnp.float32)
    for core in range(2):

        @pl.when(me_core == core)
        def _():
            at = slice(core * quarter, (core + 1) * quarter)
            params_ref[2:3, :quarter] = bqv_ref[0:1, at]
            params_ref[2:3, 2 * quarter : 3 * quarter] = bqv_ref[1:2, at]
            params_ref[6:7, :] = bfc_ref[...].reshape(1, 2 * width)[:, core * width : (core + 1) * width]


def pack(w_qkv, w_proj, w_fc, w_out):
    rows = w_fc.shape[0]
    b16 = jnp.bfloat16
    one = jax.ShapeDtypeStruct((rows, 2 * w_proj.shape[1]), b16)
    two = jax.ShapeDtypeStruct((rows, w_fc.shape[1]), b16)
    return pl.pallas_call(
        pack_kernel,
        out_shape=(one, one, two, two),
        in_specs=[HBM] * 4,
        out_specs=[VMEM] * 4,
        scratch_shapes=[
            pltpu.VMEM(w_qkv.shape, b16),
            pltpu.VMEM(w_proj.shape, b16),
            pltpu.SemaphoreType.DMA((6,)),
        ],
        compiler_params=pltpu.CompilerParams(vmem_limit_bytes=63 << 20),
    )(w_qkv, w_proj, w_fc, w_out)


def setting_kernel(*refs, quarter, chips):
    vectors, table_ref, params_ref = refs[:-2], refs[-2], refs[-1]
    core = lax.rem(lax.axis_index("dp"), 2)
    if chips:
        fill_table(table_ref, chips)
    else:
        table_ref[CORE] = core
        table_ref[SIDE] = lax.axis_index("tensor")
        table_ref[2] = 0
    fill_params(core, vectors, params_ref, quarter)


def setting(vectors, quarter, chips):
    table = jax.ShapeDtypeStruct((table_size(chips) if chips else 3,), jnp.int32)
    params = jax.ShapeDtypeStruct((8, vectors[0].shape[0]), jnp.float32)
    return pl.pallas_call(
        functools.partial(setting_kernel, quarter=quarter, chips=chips),
        out_shape=(table, params),
        in_specs=[VMEM] * len(vectors),
        out_specs=[SMEM, VMEM],
        compiler_params=pltpu.CompilerParams(vmem_limit_bytes=4 << 20),
    )(*vectors)


def own_pair_kernel(count_ref, x_ref, grad_ref, pair_ref):
    rows = x_ref.shape[0]
    line = lax.broadcasted_iota(jnp.int32, (rows, 1), 0) + lax.axis_index("tensor") * rows
    live = (line < count_ref[0]).astype(jnp.float32)
    pair_ref[0] = x_ref[...]
    pair_ref[1] = bf(grad_ref[...].astype(jnp.float32) * live)


def block_out_kernel(count_ref, resid_ref, own_ref, met_ref, params_ref, out_ref):
    rows = out_ref.shape[0]
    line = lax.broadcasted_iota(jnp.int32, (rows, 1), 0) + lax.axis_index("tensor") * rows
    live = (line < count_ref[0]).astype(jnp.float32)
    total = own_ref[...] + met_ref[...].astype(jnp.float32)
    out_ref[...] = bf((resid_ref[...] + total + params_ref[7:8, :]) * live)


def finish_one_kernel(core_ref, keep_ref, other_ref, qkv_ref, proj_ref, sums_ref, fc_ref, qv_ref):
    rows = proj_ref.shape[0]
    quarter = proj_ref.shape[1] // 2
    width = keep_ref.shape[1]
    sums_ref[...] = keep_ref[rows : rows + 8, :] + other_ref[rows : rows + 8, :]
    for core in range(2):

        @pl.when(core_ref[CORE] == core)
        def _():
            for ref, part in ((keep_ref, core), (other_ref, 1 - core)):
                at = slice(part * quarter, (part + 1) * quarter)
                for which in range(3):
                    qkv_ref[which, :, at] = ref[:rows, which * quarter : (which + 1) * quarter]
                proj_ref[:, at] = ref[:rows, 3 * quarter :]
                fc_ref[pl.ds(part * width, width)] = ref[rows + 6 : rows + 7, :].reshape(width)
                qv_ref[0:1, at] = ref[rows + 7 : rows + 8, :quarter]
                qv_ref[1:2, at] = ref[rows + 7 : rows + 8, quarter : 2 * quarter]


def finish_one(table, keep, other, rows):
    width = keep.shape[1]
    f32 = jnp.float32
    outs = (
        jax.ShapeDtypeStruct((3, rows, width // 2), f32),
        jax.ShapeDtypeStruct((rows, width // 2), f32),
        jax.ShapeDtypeStruct((8, width), f32),
        jax.ShapeDtypeStruct((2 * width,), f32),
        jax.ShapeDtypeStruct((2, width // 2), f32),
    )
    return ring_call(finish_one_kernel, outs, table, keep, other)


def finish_two_kernel(core_ref, keep_ref, other_ref, fc_ref, out_ref):
    hidden = keep_ref.shape[1] // 2
    for core in range(2):

        @pl.when(core_ref[CORE] == core)
        def _():
            for ref, part in ((keep_ref, core), (other_ref, 1 - core)):
                at = slice(part * hidden, (part + 1) * hidden)
                fc_ref[:, at] = ref[:, :hidden]
                out_ref[:, at] = ref[:, hidden:]


def finish_two(table, keep, other):
    out = jax.ShapeDtypeStruct(keep.shape, jnp.float32)
    return ring_call(finish_two_kernel, (out, out), table, keep, other)


def core_part(array, core, axis):
    width = array.shape[axis] // 2
    return lax.dynamic_slice_in_dim(array, core * width, width, axis=axis)


def swap_halves(rows):
    half = rows.shape[0] // 2
    return jnp.concatenate([rows[half:], rows[:half]], axis=0)


def rows_to_owners(kept, sent):
    rows, width = kept.shape[0] // 2, kept.shape[1]
    met = core_swap(sent)
    outs = (
        jax.ShapeDtypeStruct((rows, width), jnp.float32),
        jax.ShapeDtypeStruct((rows, width), jnp.bfloat16),
    )
    own, other = pl.pallas_call(
        pair_kernel,
        out_shape=outs,
        in_specs=[VMEM] * 2,
        out_specs=[VMEM] * 2,
        compiler_params=pltpu.CompilerParams(vmem_limit_bytes=8 << 20),
        cost_estimate=pl.CostEstimate(flops=0, bytes_accessed=1 << 20, transcendentals=0),
    )(kept, met)
    return own, x_swap(other)


def dot(left, right, left_dim, right_dim):
    return lax.dot_general(
        left, right, (((left_dim,), (right_dim,)), ((), ())), preferred_element_type=jnp.float32
    )


def join_kernel(p0_ref, p1_ref, p2_ref, p3_ref, x_ref, g_ref):
    rows = p0_ref.shape[1]
    for block, pair_ref in enumerate((p0_ref, p1_ref, p2_ref, p3_ref)):
        x_ref[pl.ds(block * rows, rows), :] = pair_ref[0]
        g_ref[pl.ds(block * rows, rows), :] = pair_ref[1]


def join(pairs):
    rows, width = pairs[0].shape[1:]
    out = jax.ShapeDtypeStruct((4 * rows, width), jnp.bfloat16)
    return pl.pallas_call(
        join_kernel,
        out_shape=(out, out),
        in_specs=[VMEM] * 4,
        out_specs=[VMEM] * 2,
        compiler_params=pltpu.CompilerParams(vmem_limit_bytes=8 << 20),
        cost_estimate=pl.CostEstimate(flops=0, bytes_accessed=3 << 20, transcendentals=0),
    )(*pairs)


def attention_kernel(info_ref, w_ref, x_ref, seg_ref, params_ref, *refs, saving):
    if saving:
        normed_ref, hat_ref, qkv_ref, prob_ref, mixed_ref = refs
    else:
        mixed_ref, normed_ref, qkv_ref = refs
    side = info_ref[SIDE]
    rows = x_ref.shape[0] // 4
    group = 2 * rows
    three = qkv_ref.shape[1]
    quarter = three // 3
    heads = quarter // HD
    for block in range(4):
        here = pl.ds(block * rows, rows)
        hat, _ = normalize(x_ref[here, :].astype(jnp.float32))
        if saving:
            hat_ref[here, :] = hat
        normed_ref[here, :] = bf(hat * params_ref[0:1, :] + params_ref[1:2, :])
    qkv_ref[...] = bf(dot(normed_ref[...], w_ref[:, :three], 1, 0) + params_ref[2:3, :three])
    down = lax.broadcasted_iota(jnp.int32, (group, group), 0) + side * rows
    across = lax.broadcasted_iota(jnp.int32, (group, group), 1) + side * rows
    down = jnp.where(down >= group, down - group, down)
    across = jnp.where(across >= group, across - group, across)
    causal = across <= down
    for index in range(2):
        seg = seg_ref[pl.ds(index, 1), :]
        turned = jnp.concatenate([seg[:, rows:], seg[:, :rows]], axis=1)
        seg_across = jnp.broadcast_to(jnp.where(side == 0, seg, turned), (group, group))
        allowed = causal & (seg_across == seg_across.T)
        part = pl.ds(index * group, group)
        for head in range(heads):
            query = qkv_ref[part, head * HD : (head + 1) * HD]
            keys = qkv_ref[part, quarter + head * HD : quarter + (head + 1) * HD]
            values = qkv_ref[part, 2 * quarter + head * HD : 2 * quarter + (head + 1) * HD]
            scores = dot(query, keys, 1, 1) * SCALE
            exp_scores = jnp.where(allowed, jnp.exp(scores), 0.0)
            prob = exp_scores / jnp.sum(exp_scores, axis=-1, keepdims=True)
            mixed = bf(dot(bf(prob), values, 1, 0))
            if saving:
                prob_ref[index * heads + head] = prob
                mixed_ref[part, head * HD : (head + 1) * HD] = mixed
            else:
                for half in range(2):
                    start = (2 * index + half) * quarter + head * HD
                    mixed_ref[:, start : start + HD] = mixed[half * rows : (half + 1) * rows]


def attention(info, w_full, x_all, segs, params, saving):
    rows, width = x_all.shape[0] // 4, x_all.shape[1]
    three = 3 * width // 4
    heads = three // 3 // HD
    f32, b16 = jnp.float32, jnp.bfloat16
    normed, joined = ((4 * rows, width), b16), ((4 * rows, three), b16)
    if saving:
        outs = [
            normed,
            ((4 * rows, width), f32),
            joined,
            ((2 * heads, 2 * rows, 2 * rows), f32),
            ((4 * rows, three // 3), b16),
        ]
    else:
        outs = [((rows, 4 * three // 3), b16)]
    ins = (w_full, x_all, segs, params)
    return pl.pallas_call(
        functools.partial(attention_kernel, saving=saving),
        out_shape=[jax.ShapeDtypeStruct(*one) for one in outs],
        in_specs=[SMEM] + [VMEM] * len(ins),
        out_specs=[VMEM] * len(outs),
        scratch_shapes=[] if saving else [pltpu.VMEM(*normed), pltpu.VMEM(*joined)],
        compiler_params=pltpu.CompilerParams(vmem_limit_bytes=16 << 20),
        cost_estimate=pl.CostEstimate(flops=1 << 30, bytes_accessed=8 << 20, transcendentals=400000),
    )(info, *ins)


def mlp_kernel(index_ref, *refs, piece_count):
    pieces, refs = refs[:piece_count], refs[piece_count:]
    (m0_ref, m1_ref, m2_ref, m3_ref, p0_ref, p1_ref, p2_ref, p3_ref, x_ref, g_ref, params_ref,
     resid_ref, hat_ref, inv_ref, normed_ref, act_ref, grad_ref, keep_ref, send_ref, sums_ref, out_ref,
     fc_ref, wide_ref, slope_ref, proj_ref, mixed_ref, sems) = refs
    copies = fill(index_ref, pieces, (fc_ref, out_ref), sems)
    rows = m0_ref.shape[0]
    quarter = p0_ref.shape[0]
    for source, (m_ref, p_ref) in enumerate(
        ((m0_ref, p0_ref), (m1_ref, p1_ref), (m2_ref, p2_ref), (m3_ref, p3_ref))
    ):
        at = slice(source * quarter, (source + 1) * quarter)
        for block in range(4):
            start = (block ^ source) * quarter
            mixed_ref[pl.ds(block * rows, rows), at] = m_ref[:, start : start + quarter]
            proj_ref[pl.ds(block * quarter, quarter), at] = p_ref[
                :, block * quarter : (block + 1) * quarter
            ]
    wide_ref[...] = dot(mixed_ref[...], proj_ref[...], 1, 1)
    for block in range(4):
        here = pl.ds(block * rows, rows)
        resid = wide_ref[here, :] + x_ref[here, :].astype(jnp.float32) + params_ref[3:4, :]
        if block == 0:
            resid_ref[...] = resid
        hat, inv = normalize(resid)
        hat_ref[here, :] = hat
        inv_ref[here, :] = jnp.broadcast_to(inv, (rows, inv_ref.shape[1]))
        normed_ref[here, :] = bf(hat * params_ref[4:5, :] + params_ref[5:6, :])
    for copy in copies:
        copy.wait()
    wide_ref[...] = dot(normed_ref[...], fc_ref[...], 1, 0)
    for block in range(4):
        here = pl.ds(block * rows, rows)
        act_value, act_slope = gelu_parts(wide_ref[here, :] + params_ref[6:7, :])
        act_ref[here, :] = bf(act_value)
        slope_ref[here, :] = act_slope
    wide_ref[...] = dot(g_ref[...], out_ref[...], 1, 0)
    total = jnp.zeros((1, act_ref.shape[1]), jnp.float32)
    for block in range(4):
        here = pl.ds(block * rows, rows)
        grad_pre = wide_ref[here, :] * slope_ref[here, :]
        total += jnp.sum(grad_pre, axis=0, keepdims=True)
        grad_ref[here, :] = bf(grad_pre)
    sums_ref[...] = jnp.broadcast_to(total, sums_ref.shape)
    part = dot(grad_ref[...], fc_ref[...], 1, 1)
    keep_ref[...] = part[: 2 * rows]
    send_ref[...] = bf(part[2 * rows :])


def mlp(index, pieces, mixed_parts, proj_parts, x_all, grad_all, params, count):
    all_rows, width = x_all.shape
    hidden = pieces[0].shape[1] // 2
    f32, b16 = jnp.float32, jnp.bfloat16
    outs = (
        ((all_rows // 4, width), f32),
        ((all_rows, width), f32),
        ((all_rows, 128), f32),
        ((all_rows, width), b16),
        ((all_rows, hidden), b16),
        ((all_rows, hidden), b16),
        ((all_rows // 2, width), f32),
        ((all_rows // 2, width), b16),
        ((8, hidden), f32),
        ((width, hidden), b16),
    )
    ins = (*mixed_parts, *proj_parts, x_all, grad_all, params)
    return pl.pallas_call(
        functools.partial(mlp_kernel, piece_count=len(pieces)),
        out_shape=[jax.ShapeDtypeStruct(*one) for one in outs],
        in_specs=[SMEM] + [pl.BlockSpec(memory_space=pl.ANY)] * len(pieces) + [VMEM] * len(ins),
        out_specs=[VMEM] * len(outs),
        scratch_shapes=[
            pltpu.VMEM((width, hidden), b16),
            pltpu.VMEM((all_rows, width), f32),
            pltpu.VMEM((all_rows, width), f32),
            pltpu.VMEM((width, width), b16),
            pltpu.VMEM((all_rows, width), b16),
            pltpu.SemaphoreType.DMA((2 * count,)),
        ],
        compiler_params=pltpu.CompilerParams(vmem_limit_bytes=VMEM_LIMIT),
        cost_estimate=pl.CostEstimate(flops=3 << 30, bytes_accessed=12 << 20, transcendentals=400000),
    )(index, *pieces, *ins)


def back_kernel(
    table_ref, own_ref, other_ref, fc_sums_ref, params_ref, g_ref, hat_ref, inv_ref, w_ref, qkv_ref, prob_ref,
    normed_ref, one_ref, mixed_ref,
    d_one_ref, keep_ref, send_ref, resid_ref, sums_ref, ahead_ref, back_ref, joined_ref, resid_bf,
    grad_mixed, *, chips,
):
    rows, width = resid_ref.shape
    group = 2 * rows
    three = qkv_ref.shape[1]
    quarter = three // 3
    heads = quarter // HD
    for block in range(4):
        here = pl.ds(block * rows, rows)
        if block < 2:
            grad = own_ref[here, :]
        else:
            grad = other_ref[pl.ds((block - 2) * rows, rows), :].astype(jnp.float32)
        hat = hat_ref[here, :]
        live_grad = g_ref[here, :].astype(jnp.float32)
        grad_resid = live_grad + norm_back(grad, params_ref[4:5, :], hat, inv_ref[here, 0:1])
        resid_bf[here, :] = bf(grad_resid)
        if block == 0:
            resid_ref[...] = grad_resid
            sums_ref[2:3, :] = jnp.sum(grad * hat, axis=0, keepdims=True)
            sums_ref[3:4, :] = jnp.sum(grad, axis=0, keepdims=True)
            sums_ref[4:5, :] = jnp.sum(grad_resid, axis=0, keepdims=True)
            sums_ref[5:6, :] = jnp.sum(live_grad, axis=0, keepdims=True)
    sums_ref[6:7, :] = fc_sums_ref[0:1, :]
    sums_ref[7:8, :] = jnp.zeros((1, width), jnp.float32)
    grad_mixed[...] = bf(dot(resid_bf[...], w_ref[:, three:], 1, 0))
    for head in range(heads):
        at_q = slice(head * HD, (head + 1) * HD)
        at_k = slice(quarter + head * HD, quarter + (head + 1) * HD)
        at_v = slice(2 * quarter + head * HD, 2 * quarter + (head + 1) * HD)
        sum_q = jnp.zeros((1, HD), jnp.float32)
        sum_v = jnp.zeros((1, HD), jnp.float32)
        for index in range(2):
            part = pl.ds(index * group, group)
            prob = prob_ref[index * heads + head]
            mixed_grad = grad_mixed[part, at_q]
            grad_prob = dot(mixed_grad, qkv_ref[part, at_v], 1, 1)
            delta = jnp.sum(prob * grad_prob, axis=-1, keepdims=True)
            grad_scores = bf(prob * (grad_prob - delta) * SCALE)
            grad_query = dot(grad_scores, qkv_ref[part, at_k], 1, 0)
            grad_key = dot(grad_scores, qkv_ref[part, at_q], 0, 0)
            grad_value = dot(bf(prob), mixed_grad, 0, 0)
            sum_q += jnp.sum(grad_query, axis=0, keepdims=True)
            sum_v += jnp.sum(grad_value, axis=0, keepdims=True)
            joined_ref[part, at_q] = bf(grad_query)
            joined_ref[part, at_k] = bf(grad_key)
            joined_ref[part, at_v] = bf(grad_value)
        sums_ref[7:8, at_q] = sum_q
        sums_ref[7:8, at_k] = sum_v
    whole = dot(joined_ref[...], w_ref[:, :three], 1, 1)
    with_hat = jnp.zeros((1, width), jnp.float32)
    plain = jnp.zeros((1, width), jnp.float32)
    for block in range(4):
        part = whole[block * rows : (block + 1) * rows]
        with_hat += jnp.sum(part * one_ref[pl.ds(block * rows, rows), :], axis=0, keepdims=True)
        plain += jnp.sum(part, axis=0, keepdims=True)
    keep_ref[...] = whole[:group]
    send_ref[...] = bf(whole[group:])
    sums_ref[0:1, :] = with_hat
    sums_ref[1:2, :] = plain
    parts = (
        bf(dot(normed_ref[...], joined_ref[...], 0, 0)),
        bf(dot(resid_bf[...], mixed_ref[...], 0, 0)),
    )
    count = width // chips
    half = count // 2
    shared = d_one_ref.shape[0] // chips - count
    if shared:
        sums = sums_ref[...]
        sums = bf(jnp.concatenate([sums, jnp.zeros_like(sums)], axis=0))
    for chip in range(chips):
        start = chip * (count + shared)
        for part, at in zip(parts, (slice(0, three), slice(three, width))):
            d_one_ref[start : start + half, at] = part[chip * count : chip * count + half]
            d_one_ref[start + half + shared : start + count + shared, at] = part[
                chip * count + half : (chip + 1) * count
            ]
        if shared:
            d_one_ref[start + half : start + half + shared, :] = sums
    if shared:
        send_far(table_ref, d_one_ref, ahead_ref, back_ref)


def back(table, h2_own, h2_other, fc_sums, params, saved, chips, shared):
    all_rows, width = saved[0].shape
    f32, b16 = jnp.float32, jnp.bfloat16
    quarter = width // 4
    outs = (
        ((width + chips * shared, width), b16),
        ((all_rows // 2, width), f32),
        ((all_rows // 2, width), b16),
        ((all_rows // 4, width), f32),
        ((8, width), f32),
        ((width // chips // 2 + shared, width), b16),
        ((width // chips // 2, width), b16),
    )
    ins = (h2_own, h2_other, fc_sums, params, *saved)
    return pl.pallas_call(
        functools.partial(back_kernel, chips=chips),
        out_shape=[jax.ShapeDtypeStruct(*one) for one in outs],
        in_specs=[SMEM] + [VMEM] * len(ins),
        out_specs=[VMEM] * len(outs),
        scratch_shapes=[
            pltpu.VMEM((all_rows, 3 * quarter), b16),
            pltpu.VMEM((all_rows, width), b16),
            pltpu.VMEM((all_rows, quarter), b16),
        ],
        compiler_params=pltpu.CompilerParams(vmem_limit_bytes=VMEM_LIMIT),
        cost_estimate=pl.CostEstimate(flops=2 << 30, bytes_accessed=10 << 20, transcendentals=0),
    )(table, *ins)


def weights_two_kernel(table_ref, normed_ref, grad_ref, g_ref, act_ref, out_ref, *far_refs):
    hidden = act_ref.shape[1]
    out_ref[:, :hidden] = bf(dot(normed_ref[...], grad_ref[...], 0, 0))
    out_ref[:, hidden:] = bf(dot(g_ref[...], act_ref[...], 0, 0))
    if far_refs:
        send_far(table_ref, out_ref, *far_refs)


def weights_two(table, normed, grad, grad_all, act, far_rows):
    ins = (normed, grad, grad_all, act)
    b16 = jnp.bfloat16
    out = jax.ShapeDtypeStruct((normed.shape[1], 2 * act.shape[1]), b16)
    far = jax.ShapeDtypeStruct((far_rows, 2 * act.shape[1]), b16)
    outs = (out, far, far) if far_rows else (out,)
    return pl.pallas_call(
        weights_two_kernel,
        out_shape=outs,
        in_specs=[SMEM] + [VMEM] * len(ins),
        out_specs=[VMEM] * len(outs),
        compiler_params=pltpu.CompilerParams(vmem_limit_bytes=VMEM_LIMIT),
        cost_estimate=pl.CostEstimate(flops=1 << 30, bytes_accessed=4 << 20, transcendentals=0),
    )(table, *ins)


def mlp_out_kernel(act_ref, w_ref, keep_ref, send_ref):
    half = keep_ref.shape[0]
    part = dot(act_ref[...], w_ref[...], 1, 1)
    keep_ref[...] = part[:half]
    send_ref[...] = bf(part[half:])


def mlp_out(act, w_out):
    rows, width = act.shape[0] // 2, w_out.shape[0]
    return pl.pallas_call(
        mlp_out_kernel,
        out_shape=(
            jax.ShapeDtypeStruct((rows, width), jnp.float32),
            jax.ShapeDtypeStruct((rows, width), jnp.bfloat16),
        ),
        in_specs=[VMEM] * 2,
        out_specs=[VMEM] * 2,
        compiler_params=pltpu.CompilerParams(vmem_limit_bytes=8 << 20),
        cost_estimate=pl.CostEstimate(flops=1 << 29, bytes_accessed=3 << 20, transcendentals=0),
    )(act, w_out)


def inputs_kernel(x_ref, keep_ref, met_ref, resid_ref, params_ref, out_ref):
    hat, inv = normalize(x_ref[...].astype(jnp.float32))
    grad = keep_ref[...] + met_ref[...].astype(jnp.float32)
    out_ref[...] = bf(resid_ref[...] + norm_back(grad, params_ref[0:1, :], hat, inv))


def grad_inputs(tokens, kept, met, resid, params):
    ins = (tokens, kept, met, resid, params)
    return pl.pallas_call(
        inputs_kernel,
        out_shape=jax.ShapeDtypeStruct(tokens.shape, jnp.bfloat16),
        in_specs=[VMEM] * len(ins),
        out_specs=VMEM,
        compiler_params=pltpu.CompilerParams(vmem_limit_bytes=8 << 20),
        cost_estimate=pl.CostEstimate(flops=0, bytes_accessed=1 << 20, transcendentals=0),
    )(*ins)


def pair_kernel(keep_ref, met_ref, own_ref, send_ref):
    rows = own_ref.shape[0]
    pair = keep_ref[...] + met_ref[...].astype(jnp.float32)
    own_ref[...] = pair[:rows]
    send_ref[...] = bf(pair[rows:])


def block(
    tokens,
    segment_ids,
    valid_counts,
    ln1_gain,
    ln1_bias,
    w_qkv,
    b_qv,
    w_proj,
    b_proj,
    ln2_gain,
    ln2_bias,
    w_fc,
    b_fc,
    w_out,
    b_out,
    grad_out,
):
    me = lax.axis_index("dp")
    core = me % 2
    _, width = tokens.shape
    shard_rows = w_fc.shape[0]
    quarter = w_qkv.shape[2] // 2

    def chip_rows(kept, sent):
        return jnp.concatenate([kept, core_swap(sent)], axis=0)

    ring = use_ring(shard_rows)
    chips = lax.axis_size("dp") // 2
    rows_out = jax.ShapeDtypeStruct(tokens.shape, jnp.bfloat16)
    pair_out = jax.ShapeDtypeStruct((2,) + tokens.shape, jnp.bfloat16)
    (own_pair,) = ring_call(own_pair_kernel, (pair_out,), valid_counts, tokens, grad_out)
    vectors = (ln1_gain, ln1_bias, b_qv, b_proj, ln2_gain, ln2_bias, b_fc, b_out)
    table, params = setting(vectors, quarter, chips if ring else 0)
    if ring:
        keep_one, send_one, keep_two, send_two = pack(w_qkv, w_proj, w_fc, w_out)
        one_pieces = gather_rows(chip_rows(keep_one, send_one))
        two_pieces = gather_rows(chip_rows(keep_two, send_two))
        blocks = 2 * chips
    else:
        blocks = 1
        full_four = [
            core_part(lax.all_gather(shard, "dp", axis=0, tiled=True), core, 1)
            for shard in (w_qkv[0], w_qkv[1], w_qkv[2], w_proj, w_fc, w_out)
        ]
        one_pieces = [jnp.concatenate(full_four[:4], axis=1)]
        two_pieces = [jnp.concatenate(full_four[4:], axis=1)]
    x_pair = x_swap(own_pair)
    core_pair = core_swap(own_pair)
    far_pair = core_swap(x_pair)
    x_all, grad_all = join((own_pair, x_pair, core_pair, far_pair))
    segs = jnp.stack([segment_ids, core_swap(segment_ids)])

    one_full, proj_own = assemble_one(table, one_pieces, width, blocks)
    proj_x = x_swap(proj_own)
    mixed = attention(table, one_full, x_all, segs, params, False)[0]
    proj_c, proj_cx = core_swap(proj_own), core_swap(proj_x)
    mixed_x = x_swap(mixed)
    mixed_c, mixed_cx = core_swap(mixed), core_swap(mixed_x)
    (
        resid_own_one, hat_two, inv_two, normed_two, act_bf, grad_pre_bf, h2_keep, h2_send, fc_sums,
        out_full,
    ) = mlp(
        table,
        two_pieces,
        (mixed, mixed_x, mixed_c, mixed_cx),
        (proj_own, proj_x, proj_c, proj_cx),
        x_all,
        grad_all,
        params,
        blocks,
    )
    h2_pair = h2_keep + core_swap(h2_send).astype(jnp.float32)
    h2_own = h2_pair + swap_halves(x_swap(bf(h2_pair))).astype(jnp.float32)
    h2_other = core_swap(bf(h2_own))
    d_two_terms, *far = weights_two(
        table, normed_two, grad_pre_bf, grad_all, act_bf, shard_rows if ring else 0
    )
    if ring:
        kept, other = reduce_ring(table, d_two_terms, far, shard_rows)
        d_fc, d_out = finish_two(table, kept, other)
    else:
        kept, other = reduce_plain(d_two_terms)
        d_fc, d_out = (
            jnp.concatenate(
                [jnp.where(core == 0, mine, theirs), jnp.where(core == 0, theirs, mine)], axis=1
            )
            for mine, theirs in zip(jnp.split(kept, 2, axis=1), jnp.split(other, 2, axis=1))
        )
    mlp_keep, mlp_send = mlp_out(act_bf, out_full)
    mlp_own, mlp_met = rows_to_owners(mlp_keep, mlp_send)
    (block_out,) = ring_call(
        block_out_kernel, (rows_out,), valid_counts, resid_own_one, mlp_own, mlp_met, params
    )

    shared = 16 if ring else 0
    normed_one, hat_one, qkv, prob, mixed_own = attention(
        table, one_full, x_all, segs, params, True
    )
    saved = (grad_all, hat_two, inv_two, one_full, qkv, prob, normed_one, hat_one, mixed_own)
    d_one_terms, h1_keep, h1_send, resid_own, sums, *far = back(
        table, h2_own, h2_other, fc_sums, params, saved, chips if ring else 1, shared
    )
    if ring:
        kept, other = reduce_ring(table, d_one_terms, far, shard_rows)
        d_qkv, d_proj, sums, d_bfc, d_qv = finish_one(table, kept, other, shard_rows)
    else:
        reach = 2
        while reach < lax.axis_size("dp"):
            pairs_now = [(i, i ^ reach) for i in range(lax.axis_size("dp"))]
            sums = sums + lax.ppermute(sums, "dp", pairs_now)
            reach *= 2
        met = core_swap(sums)
        low, high = jnp.where(core == 0, sums, met), jnp.where(core == 0, met, sums)
        sums = sums + met
        d_bfc = jnp.concatenate([low[6], high[6]])
        d_qv = jnp.concatenate(
            [rows[7, : 2 * quarter].reshape(2, quarter) for rows in (low, high)], axis=1
        )
        kept, other = reduce_plain(d_one_terms)
        low, high = jnp.where(core == 0, kept, other), jnp.where(core == 0, other, kept)
        d_four = jnp.concatenate(
            [rows.reshape(shard_rows, 4, quarter) for rows in (low, high)], axis=2
        ).transpose(1, 0, 2)
        d_qkv, d_proj = d_four[:3], d_four[3]
    sums = sums + x_swap(sums)
    h1_own, h1_met = rows_to_owners(h1_keep, h1_send)
    grad_input = grad_inputs(tokens, h1_own, h1_met, resid_own, params)
    return (
        block_out,
        grad_input,
        sums[0],
        sums[1],
        d_qkv,
        d_qv,
        d_proj,
        sums[4],
        sums[2],
        sums[3],
        d_fc,
        d_bfc,
        d_out,
        sums[5],
    )


def solution(mesh):
    return jax.shard_map(
        block,
        mesh=mesh,
        in_specs=(
            P(("dp", "tensor"), None),
            P("dp"),
            P("dp"),
            P(),
            P(),
            P(None, "dp", "tensor"),
            P(None, "tensor"),
            P("dp", "tensor"),
            P(),
            P(),
            P(),
            P("dp", "tensor"),
            P("tensor"),
            P("dp", "tensor"),
            P(),
            P(("dp", "tensor"), None),
        ),
        out_specs=(
            P(("dp", "tensor"), None),
            P(("dp", "tensor"), None),
            P(),
            P(),
            P(None, "dp", "tensor"),
            P(None, "tensor"),
            P("dp", "tensor"),
            P(),
            P(),
            P(),
            P("dp", "tensor"),
            P("tensor"),
            P("dp", "tensor"),
            P(),
        ),
        check_vma=False,
    )
```

```python
import functools

import jax
import jax.numpy as jnp
from jax import lax
from jax.experimental import pallas as pl
from jax.experimental.pallas import tpu as pltpu
from jax.sharding import PartitionSpec as P


HD = 64


SCALE = 0.125
EPSILON = 1e-05
GELU_C = 0.7978845608028654

VMEM_LIMIT = 20 << 20
VMEM = pl.BlockSpec(memory_space=pltpu.VMEM)
SMEM = pl.BlockSpec(memory_space=pltpu.SMEM)
HBM = pl.BlockSpec(memory_space=pltpu.HBM)


def normalize(row_data):
    mean_rows = jnp.mean(row_data, axis=-1, keepdims=True)
    centred = row_data - mean_rows
    inv_std = lax.rsqrt(jnp.mean(centred * centred, axis=-1, keepdims=True) + EPSILON)
    return (centred * inv_std, inv_std)


def norm_back(grad_rows, gain_vec, normed, inv_std):
    scaled = grad_rows * gain_vec
    return inv_std * (
        scaled
        - jnp.mean(scaled, axis=-1, keepdims=True)
        - normed * jnp.mean(scaled * normed, axis=-1, keepdims=True)
    )


def gelu_parts(pre_act):
    tanh_arg = GELU_C * (pre_act + 0.044715 * pre_act * pre_act * pre_act)
    tanh_val = jnp.tanh(tanh_arg)
    act_value = 0.5 * pre_act * (1.0 + tanh_val)
    act_slope = 0.5 * (1.0 + tanh_val) + 0.5 * pre_act * (1.0 - tanh_val * tanh_val) * GELU_C * (
        1.0 + 3.0 * 0.044715 * pre_act * pre_act
    )
    return (act_value, act_slope)


def bf(value):
    return value.astype(jnp.bfloat16)


def core_swap(value):
    count = lax.axis_size("dp")
    return lax.ppermute(value, "dp", [(i, i ^ 1) for i in range(count)])


def x_swap(value):
    return lax.ppermute(value, "tensor", [(0, 1), (1, 0)])


def use_ring(shard_rows):
    return lax.axis_size("dp") <= 16 and shard_rows % 16 == 0


def ring_chips(chip_count):
    return list(range(0, chip_count, 2)) + list(range(1, chip_count, 2))[::-1]


def ring_send(value, step):
    chips = ring_chips(lax.axis_size("dp") // 2)
    size = len(chips)
    pairs = []
    for place, chip in enumerate(chips):
        other = chips[(place + step) % size]
        pairs += [(2 * chip, 2 * other), (2 * chip + 1, 2 * other + 1)]
    return lax.ppermute(value, "dp", pairs)


CORE, SIDE, CHIP, FAR, STEPS = 0, 1, 2, 3, 4


def table_size(chips):
    return 4 + 2 * (chips // 2) + 2 * chips


def fill_table(table_ref, chips):
    def chip_at(place):
        place = lax.rem(place + chips, chips)
        return jnp.where(place < chips // 2, 2 * place, 2 * (chips - 1 - place) + 1)

    me = lax.axis_index("dp")
    core, chip = lax.rem(me, 2), lax.div(me, 2)
    place = jnp.where(lax.rem(chip, 2) == 0, lax.div(chip, 2), chips - 1 - lax.div(chip, 2))
    table_ref[CORE] = core
    table_ref[SIDE] = lax.axis_index("tensor")
    table_ref[CHIP] = chip
    table_ref[FAR] = chip_at(place + chips // 2)
    entry = STEPS
    for step in range(1, chips // 2 + 1):
        table_ref[entry] = chip_at(place + step)
        table_ref[entry + 1] = chip_at(place - step)
        entry += 2
    offsets = [0]
    for step in range(1, chips // 2):
        offsets += [-step, step]
    for offset in offsets + [chips // 2]:
        owner = chip_at(place + offset)
        table_ref[entry] = 2 * owner + core
        table_ref[entry + 1] = 2 * owner + 1 - core
        entry += 2


def fill(index_ref, pieces, outs, sems):
    count = sems.shape[0] // len(outs)
    base = index_ref.shape[0] - count
    rows = outs[0].shape[0] // count
    copies = []
    slot = 0
    for piece in pieces:
        for part in range(piece.shape[0] // rows):
            start = pl.multiple_of(index_ref[base + slot] * rows, rows)
            column = 0
            for out in outs:
                source = piece.at[pl.ds(part * rows, rows), pl.ds(column, out.shape[1])]
                copy = pltpu.make_async_copy(source, out.at[pl.ds(start, rows)], sems.at[len(copies)])
                copy.start()
                copies.append(copy)
                column += out.shape[1]
            slot += 1
    return copies


def assemble_one_kernel(index_ref, *refs):
    pieces, out_ref, proj_ref, sems = refs[:-3], refs[-3], refs[-2], refs[-1]
    for copy in fill(index_ref, pieces, (out_ref,), sems):
        copy.wait()
    quarter = proj_ref.shape[0]
    for block in range(4):
        here = slice(block * quarter, (block + 1) * quarter)
        proj_ref[:, here] = out_ref[here, 3 * quarter :]


def assemble_one(index, pieces, width, count):
    quarter = width // 4
    outs = (
        jax.ShapeDtypeStruct((width, width), jnp.bfloat16),
        jax.ShapeDtypeStruct((quarter, width), jnp.bfloat16),
    )
    return pl.pallas_call(
        assemble_one_kernel,
        out_shape=outs,
        in_specs=[SMEM] + [pl.BlockSpec(memory_space=pl.ANY)] * len(pieces),
        out_specs=[VMEM] * len(outs),
            scratch_shapes=[pltpu.SemaphoreType.DMA((count,))],
        compiler_params=pltpu.CompilerParams(vmem_limit_bytes=VMEM_LIMIT),
        cost_estimate=pl.CostEstimate(flops=0, bytes_accessed=3 << 20, transcendentals=0),
    )(index, *pieces)


def gather_rows(chip_block):
    size = lax.axis_size("dp") // 2
    half = chip_block.shape[0] // 2
    pieces = [chip_block]
    ahead = back = chip_block
    for _ in range(1, size // 2):
        ahead = ring_send(ahead, 1)
        back = ring_send(back, -1)
        pieces += [ahead, back]
    pieces.append(ring_send(ahead[:half], 1))
    pieces.append(ring_send(back[half:], -1))
    return pieces


def send_far(table_ref, full_ref, ahead_ref, back_ref):
    cut = ahead_ref.shape[0]
    rows = cut + back_ref.shape[0]
    block = full_ref[pl.ds(pl.multiple_of(table_ref[FAR] * rows, 16), rows), :]
    ahead_ref[...] = block[:cut]
    back_ref[...] = block[cut:]


def step_kernel(table_ref, full_ref, ahead_ref, back_ref, up_ref, down_ref, *, step):
    rows = up_ref.shape[0]
    head, tail = ahead_ref.shape[0], back_ref.shape[0]
    at_up, at_down = table_ref[STEPS + 2 * (step - 1)], table_ref[STEPS + 2 * (step - 1) + 1]
    up = full_ref[pl.ds(pl.multiple_of(at_up * rows, 16), rows), :]
    down = full_ref[pl.ds(pl.multiple_of(at_down * rows, 16), rows), :]
    up_ref[...] = up
    down_ref[...] = down
    up_ref[:head, :] = bf(up[:head].astype(jnp.float32) + ahead_ref[...].astype(jnp.float32))
    down_ref[rows - tail :, :] = bf(
        down[rows - tail :].astype(jnp.float32) + back_ref[...].astype(jnp.float32)
    )


def last_kernel(table_ref, full_ref, ahead_ref, back_ref, keep_ref, send_ref, *sums_refs):
    rows = ahead_ref.shape[0]
    kept = keep_ref.shape[0]
    half = rows - kept
    block = full_ref[pl.ds(pl.multiple_of(table_ref[CHIP] * rows, 16), rows), :]
    total = block.astype(jnp.float32) + ahead_ref[...].astype(jnp.float32)
    total = total + back_ref[...].astype(jnp.float32)
    for sums_ref in sums_refs:
        sums_ref[...] = total[half : half + sums_ref.shape[0]]
    for core in range(2):

        @pl.when(table_ref[CORE] == core)
        def _():
            for ref, part in ((keep_ref, core), (send_ref, 1 - core)):
                ref[:half, :] = total[:half] if part == 0 else total[kept:]
                if kept > half:
                    ref[half:, :] = total[half:kept]


def ring_call(kernel, outs, *ins):
    return pl.pallas_call(
        kernel,
        out_shape=outs,
        in_specs=[SMEM] + [VMEM] * (len(ins) - 1),
        out_specs=[VMEM] * len(outs),
        compiler_params=pltpu.CompilerParams(vmem_limit_bytes=8 << 20),
        cost_estimate=pl.CostEstimate(flops=0, bytes_accessed=1 << 20, transcendentals=0),
    )(*ins)


def reduce_ring(table, full, far, half):
    size = lax.axis_size("dp") // 2
    rows, columns = full.shape[0] // size, full.shape[1]
    ahead = ring_send(far[0], 1)
    back = ring_send(far[1], -1)
    message = jax.ShapeDtypeStruct((rows, columns), jnp.bfloat16)
    for step in range(size // 2 - 1, 0, -1):
        kernel = functools.partial(step_kernel, step=step)
        up, down = ring_call(kernel, (message, message), table, full, ahead, back)
        ahead = ring_send(up, 1)
        back = ring_send(down, -1)
    kept = jax.ShapeDtypeStruct((rows - half, columns), jnp.float32)
    shared = jax.ShapeDtypeStruct((8, columns), jnp.float32)
    outs = (kept, kept) + ((shared,) if rows > 2 * half else ())
    keep, send, *sums = ring_call(last_kernel, outs, table, full, ahead, back)
    return keep, core_swap(send), sums


def reduce_plain(full):
    device_count = lax.axis_size("dp")
    core = lax.axis_index("dp") % 2
    none = jnp.zeros_like(full)
    wide = jnp.concatenate(
        [jnp.where(core == 0, full, none), jnp.where(core == 0, none, full)], axis=1
    )
    parts = lax.all_to_all(wide, "dp", split_axis=0, concat_axis=0, tiled=True)
    rows = full.shape[0] // device_count
    total = jnp.sum(parts.astype(jnp.float32).reshape(device_count, rows, -1), axis=0)
    left, right = total[:, : full.shape[1]], total[:, full.shape[1] :]
    return jnp.where(core == 0, left, right), jnp.where(core == 0, right, left)


def pack_kernel(
    qkv_hbm, proj_hbm, fc_hbm, out_hbm, keep_one, send_one, keep_two, send_two, qkv_ref, proj_ref, sems
):
    quarter = proj_ref.shape[1] // 2
    hidden = fc_hbm.shape[1] // 2
    me_core = lax.rem(lax.axis_index("dp"), 2)
    copies = [
        pltpu.make_async_copy(qkv_hbm, qkv_ref, sems.at[0]),
        pltpu.make_async_copy(proj_hbm, proj_ref, sems.at[1]),
    ]
    for place, (two, part) in enumerate(((keep_two, me_core), (send_two, 1 - me_core))):
        for half, source in enumerate((fc_hbm, out_hbm)):
            at = pl.ds(pl.multiple_of(part * hidden, 128), hidden)
            into = two.at[:, pl.ds(half * hidden, hidden)]
            copies.append(pltpu.make_async_copy(source.at[:, at], into, sems.at[2 + 2 * place + half]))
    for copy in copies:
        copy.start()
    copies[0].wait()
    copies[1].wait()
    for core in range(2):

        @pl.when(me_core == core)
        def _():
            for one, part in ((keep_one, core), (send_one, 1 - core)):
                at = slice(part * quarter, (part + 1) * quarter)
                for which in range(3):
                    one[:, which * quarter : (which + 1) * quarter] = qkv_ref[which, :, at]
                one[:, 3 * quarter :] = proj_ref[:, at]

    for copy in copies[2:]:
        copy.wait()


def fill_params(me_core, vectors, params_ref, quarter):
    width = params_ref.shape[1]
    g1_ref, b1_ref, bqv_ref, bp_ref, g2_ref, b2_ref, bfc_ref, bo_ref = vectors
    for place, ref in ((0, g1_ref), (1, b1_ref), (3, bp_ref), (4, g2_ref), (5, b2_ref), (7, bo_ref)):
        params_ref[place : place + 1, :] = ref[...].reshape(1, width)
    params_ref[2:3, :] = jnp.zeros((1, width), jnp.float32)
    for core in range(2):

        @pl.when(me_core == core)
        def _():
            at = slice(core * quarter, (core + 1) * quarter)
            params_ref[2:3, :quarter] = bqv_ref[0:1, at]
            params_ref[2:3, 2 * quarter : 3 * quarter] = bqv_ref[1:2, at]
            params_ref[6:7, :] = bfc_ref[...].reshape(1, 2 * width)[:, core * width : (core + 1) * width]


def pack(w_qkv, w_proj, w_fc, w_out):
    rows = w_fc.shape[0]
    b16 = jnp.bfloat16
    one = jax.ShapeDtypeStruct((rows, 2 * w_proj.shape[1]), b16)
    two = jax.ShapeDtypeStruct((rows, w_fc.shape[1]), b16)
    return pl.pallas_call(
        pack_kernel,
        out_shape=(one, one, two, two),
        in_specs=[HBM] * 4,
        out_specs=[VMEM] * 4,
        scratch_shapes=[
            pltpu.VMEM(w_qkv.shape, b16),
            pltpu.VMEM(w_proj.shape, b16),
            pltpu.SemaphoreType.DMA((6,)),
        ],
        compiler_params=pltpu.CompilerParams(vmem_limit_bytes=63 << 20),
    )(w_qkv, w_proj, w_fc, w_out)


def setting_kernel(*refs, quarter, chips):
    vectors, table_ref, params_ref = refs[:-2], refs[-2], refs[-1]
    core = lax.rem(lax.axis_index("dp"), 2)
    if chips:
        fill_table(table_ref, chips)
    else:
        table_ref[CORE] = core
        table_ref[SIDE] = lax.axis_index("tensor")
        table_ref[2] = 0
    fill_params(core, vectors, params_ref, quarter)


def setting(vectors, quarter, chips):
    table = jax.ShapeDtypeStruct((table_size(chips) if chips else 3,), jnp.int32)
    params = jax.ShapeDtypeStruct((8, vectors[0].shape[0]), jnp.float32)
    return pl.pallas_call(
        functools.partial(setting_kernel, quarter=quarter, chips=chips),
        out_shape=(table, params),
        in_specs=[VMEM] * len(vectors),
        out_specs=[SMEM, VMEM],
        compiler_params=pltpu.CompilerParams(vmem_limit_bytes=4 << 20),
    )(*vectors)


def own_pair_kernel(count_ref, x_ref, grad_ref, pair_ref):
    rows = x_ref.shape[0]
    line = lax.broadcasted_iota(jnp.int32, (rows, 1), 0) + lax.axis_index("tensor") * rows
    live = (line < count_ref[0]).astype(jnp.float32)
    pair_ref[0] = x_ref[...]
    pair_ref[1] = bf(grad_ref[...].astype(jnp.float32) * live)


def block_out_kernel(count_ref, resid_ref, own_ref, met_ref, params_ref, out_ref):
    rows = out_ref.shape[0]
    line = lax.broadcasted_iota(jnp.int32, (rows, 1), 0) + lax.axis_index("tensor") * rows
    live = (line < count_ref[0]).astype(jnp.float32)
    total = own_ref[...] + met_ref[...].astype(jnp.float32)
    out_ref[...] = bf((resid_ref[...] + total + params_ref[7:8, :]) * live)


def finish_one_kernel(core_ref, keep_ref, other_ref, qkv_ref, proj_ref, sums_ref, fc_ref, qv_ref):
    rows = proj_ref.shape[0]
    quarter = proj_ref.shape[1] // 2
    width = keep_ref.shape[1]
    sums_ref[...] = keep_ref[rows : rows + 8, :] + other_ref[rows : rows + 8, :]
    for core in range(2):

        @pl.when(core_ref[CORE] == core)
        def _():
            for ref, part in ((keep_ref, core), (other_ref, 1 - core)):
                at = slice(part * quarter, (part + 1) * quarter)
                for which in range(3):
                    qkv_ref[which, :, at] = ref[:rows, which * quarter : (which + 1) * quarter]
                proj_ref[:, at] = ref[:rows, 3 * quarter :]
                fc_ref[pl.ds(part * width, width)] = ref[rows + 6 : rows + 7, :].reshape(width)
                qv_ref[0:1, at] = ref[rows + 7 : rows + 8, :quarter]
                qv_ref[1:2, at] = ref[rows + 7 : rows + 8, quarter : 2 * quarter]


def finish_one(table, keep, other, rows):
    width = keep.shape[1]
    f32 = jnp.float32
    outs = (
        jax.ShapeDtypeStruct((3, rows, width // 2), f32),
        jax.ShapeDtypeStruct((rows, width // 2), f32),
        jax.ShapeDtypeStruct((8, width), f32),
        jax.ShapeDtypeStruct((2 * width,), f32),
        jax.ShapeDtypeStruct((2, width // 2), f32),
    )
    return ring_call(finish_one_kernel, outs, table, keep, other)


def finish_two_kernel(core_ref, keep_ref, other_ref, fc_ref, out_ref):
    hidden = keep_ref.shape[1] // 2
    for core in range(2):

        @pl.when(core_ref[CORE] == core)
        def _():
            for ref, part in ((keep_ref, core), (other_ref, 1 - core)):
                at = slice(part * hidden, (part + 1) * hidden)
                fc_ref[:, at] = ref[:, :hidden]
                out_ref[:, at] = ref[:, hidden:]


def finish_two(table, keep, other):
    out = jax.ShapeDtypeStruct(keep.shape, jnp.float32)
    return ring_call(finish_two_kernel, (out, out), table, keep, other)


def core_part(array, core, axis):
    width = array.shape[axis] // 2
    return lax.dynamic_slice_in_dim(array, core * width, width, axis=axis)


def swap_halves(rows):
    half = rows.shape[0] // 2
    return jnp.concatenate([rows[half:], rows[:half]], axis=0)


def rows_to_owners(kept, sent):
    rows, width = kept.shape[0] // 2, kept.shape[1]
    met = core_swap(sent)
    outs = (
        jax.ShapeDtypeStruct((rows, width), jnp.float32),
        jax.ShapeDtypeStruct((rows, width), jnp.bfloat16),
    )
    own, other = pl.pallas_call(
        pair_kernel,
        out_shape=outs,
        in_specs=[VMEM] * 2,
        out_specs=[VMEM] * 2,
        compiler_params=pltpu.CompilerParams(vmem_limit_bytes=8 << 20),
        cost_estimate=pl.CostEstimate(flops=0, bytes_accessed=1 << 20, transcendentals=0),
    )(kept, met)
    return own, x_swap(other)


def dot(left, right, left_dim, right_dim):
    return lax.dot_general(
        left, right, (((left_dim,), (right_dim,)), ((), ())), preferred_element_type=jnp.float32
    )


def join_kernel(p0_ref, p1_ref, p2_ref, p3_ref, x_ref, g_ref):
    rows = p0_ref.shape[1]
    for block, pair_ref in enumerate((p0_ref, p1_ref, p2_ref, p3_ref)):
        x_ref[pl.ds(block * rows, rows), :] = pair_ref[0]
        g_ref[pl.ds(block * rows, rows), :] = pair_ref[1]


def join(pairs):
    rows, width = pairs[0].shape[1:]
    out = jax.ShapeDtypeStruct((4 * rows, width), jnp.bfloat16)
    return pl.pallas_call(
        join_kernel,
        out_shape=(out, out),
        in_specs=[VMEM] * 4,
        out_specs=[VMEM] * 2,
        compiler_params=pltpu.CompilerParams(vmem_limit_bytes=8 << 20),
        cost_estimate=pl.CostEstimate(flops=0, bytes_accessed=3 << 20, transcendentals=0),
    )(*pairs)


def attention_kernel(info_ref, w_ref, x_ref, seg_ref, params_ref, *refs, saving):
    if saving:
        normed_ref, hat_ref, qkv_ref, prob_ref, mixed_ref = refs
    else:
        mixed_ref, normed_ref, qkv_ref = refs
    side = info_ref[SIDE]
    rows = x_ref.shape[0] // 4
    group = 2 * rows
    three = qkv_ref.shape[1]
    quarter = three // 3
    heads = quarter // HD
    for block in range(4):
        here = pl.ds(block * rows, rows)
        hat, _ = normalize(x_ref[here, :].astype(jnp.float32))
        if saving:
            hat_ref[here, :] = hat
        normed_ref[here, :] = bf(hat * params_ref[0:1, :] + params_ref[1:2, :])
    qkv_ref[...] = bf(dot(normed_ref[...], w_ref[:, :three], 1, 0) + params_ref[2:3, :three])
    down = lax.broadcasted_iota(jnp.int32, (group, group), 0) + side * rows
    across = lax.broadcasted_iota(jnp.int32, (group, group), 1) + side * rows
    down = jnp.where(down >= group, down - group, down)
    across = jnp.where(across >= group, across - group, across)
    causal = across <= down
    for index in range(2):
        seg = seg_ref[pl.ds(index, 1), :]
        turned = jnp.concatenate([seg[:, rows:], seg[:, :rows]], axis=1)
        seg_across = jnp.broadcast_to(jnp.where(side == 0, seg, turned), (group, group))
        allowed = causal & (seg_across == seg_across.T)
        part = pl.ds(index * group, group)
        for head in range(heads):
            query = qkv_ref[part, head * HD : (head + 1) * HD]
            keys = qkv_ref[part, quarter + head * HD : quarter + (head + 1) * HD]
            values = qkv_ref[part, 2 * quarter + head * HD : 2 * quarter + (head + 1) * HD]
            scores = dot(query, keys, 1, 1) * SCALE
            exp_scores = jnp.where(allowed, jnp.exp(scores), 0.0)
            prob = exp_scores / jnp.sum(exp_scores, axis=-1, keepdims=True)
            mixed = bf(dot(bf(prob), values, 1, 0))
            if saving:
                prob_ref[index * heads + head] = prob
                mixed_ref[part, head * HD : (head + 1) * HD] = mixed
            else:
                for half in range(2):
                    start = (2 * index + half) * quarter + head * HD
                    mixed_ref[:, start : start + HD] = mixed[half * rows : (half + 1) * rows]


def attention(info, w_full, x_all, segs, params, saving):
    rows, width = x_all.shape[0] // 4, x_all.shape[1]
    three = 3 * width // 4
    heads = three // 3 // HD
    f32, b16 = jnp.float32, jnp.bfloat16
    normed, joined = ((4 * rows, width), b16), ((4 * rows, three), b16)
    if saving:
        outs = [
            normed,
            ((4 * rows, width), f32),
            joined,
            ((2 * heads, 2 * rows, 2 * rows), f32),
            ((4 * rows, three // 3), b16),
        ]
    else:
        outs = [((rows, 4 * three // 3), b16)]
    ins = (w_full, x_all, segs, params)
    return pl.pallas_call(
        functools.partial(attention_kernel, saving=saving),
        out_shape=[jax.ShapeDtypeStruct(*one) for one in outs],
        in_specs=[SMEM] + [VMEM] * len(ins),
        out_specs=[VMEM] * len(outs),
        scratch_shapes=[] if saving else [pltpu.VMEM(*normed), pltpu.VMEM(*joined)],
        compiler_params=pltpu.CompilerParams(vmem_limit_bytes=16 << 20),
        cost_estimate=pl.CostEstimate(flops=1 << 30, bytes_accessed=8 << 20, transcendentals=400000),
    )(info, *ins)


def mlp_kernel(index_ref, *refs, piece_count):
    pieces, refs = refs[:piece_count], refs[piece_count:]
    (m0_ref, m1_ref, m2_ref, m3_ref, p0_ref, p1_ref, p2_ref, p3_ref, x_ref, g_ref, params_ref,
     resid_ref, hat_ref, inv_ref, normed_ref, act_ref, grad_ref, keep_ref, send_ref, sums_ref, out_ref,
     fc_ref, wide_ref, slope_ref, proj_ref, mixed_ref, sems) = refs
    copies = fill(index_ref, pieces, (fc_ref, out_ref), sems)
    rows = m0_ref.shape[0]
    quarter = p0_ref.shape[0]
    for source, (m_ref, p_ref) in enumerate(
        ((m0_ref, p0_ref), (m1_ref, p1_ref), (m2_ref, p2_ref), (m3_ref, p3_ref))
    ):
        at = slice(source * quarter, (source + 1) * quarter)
        for block in range(4):
            start = (block ^ source) * quarter
            mixed_ref[pl.ds(block * rows, rows), at] = m_ref[:, start : start + quarter]
            proj_ref[pl.ds(block * quarter, quarter), at] = p_ref[
                :, block * quarter : (block + 1) * quarter
            ]
    wide_ref[...] = dot(mixed_ref[...], proj_ref[...], 1, 1)
    for block in range(4):
        here = pl.ds(block * rows, rows)
        resid = wide_ref[here, :] + x_ref[here, :].astype(jnp.float32) + params_ref[3:4, :]
        if block == 0:
            resid_ref[...] = resid
        hat, inv = normalize(resid)
        hat_ref[here, :] = hat
        inv_ref[here, :] = jnp.broadcast_to(inv, (rows, inv_ref.shape[1]))
        normed_ref[here, :] = bf(hat * params_ref[4:5, :] + params_ref[5:6, :])
    for copy in copies:
        copy.wait()
    wide_ref[...] = dot(normed_ref[...], fc_ref[...], 1, 0)
    for block in range(4):
        here = pl.ds(block * rows, rows)
        act_value, act_slope = gelu_parts(wide_ref[here, :] + params_ref[6:7, :])
        act_ref[here, :] = bf(act_value)
        slope_ref[here, :] = act_slope
    wide_ref[...] = dot(g_ref[...], out_ref[...], 1, 0)
    total = jnp.zeros((1, act_ref.shape[1]), jnp.float32)
    for block in range(4):
        here = pl.ds(block * rows, rows)
        grad_pre = wide_ref[here, :] * slope_ref[here, :]
        total += jnp.sum(grad_pre, axis=0, keepdims=True)
        grad_ref[here, :] = bf(grad_pre)
    sums_ref[...] = jnp.broadcast_to(total, sums_ref.shape)
    part = dot(grad_ref[...], fc_ref[...], 1, 1)
    keep_ref[...] = part[: 2 * rows]
    send_ref[...] = bf(part[2 * rows :])


def mlp(index, pieces, mixed_parts, proj_parts, x_all, grad_all, params, count):
    all_rows, width = x_all.shape
    hidden = pieces[0].shape[1] // 2
    f32, b16 = jnp.float32, jnp.bfloat16
    outs = (
        ((all_rows // 4, width), f32),
        ((all_rows, width), f32),
        ((all_rows, 128), f32),
        ((all_rows, width), b16),
        ((all_rows, hidden), b16),
        ((all_rows, hidden), b16),
        ((all_rows // 2, width), f32),
        ((all_rows // 2, width), b16),
        ((8, hidden), f32),
        ((width, hidden), b16),
    )
    ins = (*mixed_parts, *proj_parts, x_all, grad_all, params)
    return pl.pallas_call(
        functools.partial(mlp_kernel, piece_count=len(pieces)),
        out_shape=[jax.ShapeDtypeStruct(*one) for one in outs],
        in_specs=[SMEM] + [pl.BlockSpec(memory_space=pl.ANY)] * len(pieces) + [VMEM] * len(ins),
        out_specs=[VMEM] * len(outs),
        scratch_shapes=[
            pltpu.VMEM((width, hidden), b16),
            pltpu.VMEM((all_rows, width), f32),
            pltpu.VMEM((all_rows, width), f32),
            pltpu.VMEM((width, width), b16),
            pltpu.VMEM((all_rows, width), b16),
            pltpu.SemaphoreType.DMA((2 * count,)),
        ],
        compiler_params=pltpu.CompilerParams(vmem_limit_bytes=VMEM_LIMIT),
        cost_estimate=pl.CostEstimate(flops=3 << 30, bytes_accessed=12 << 20, transcendentals=400000),
    )(index, *pieces, *ins)


def back_kernel(
    table_ref, own_ref, other_ref, fc_sums_ref, params_ref, g_ref, hat_ref, inv_ref, w_ref, qkv_ref, prob_ref,
    normed_ref, one_ref, mixed_ref,
    d_one_ref, keep_ref, send_ref, resid_ref, sums_ref, ahead_ref, back_ref, joined_ref, resid_bf,
    grad_mixed, *, chips,
):
    rows, width = resid_ref.shape
    group = 2 * rows
    three = qkv_ref.shape[1]
    quarter = three // 3
    heads = quarter // HD
    for block in range(4):
        here = pl.ds(block * rows, rows)
        if block < 2:
            grad = own_ref[here, :]
        else:
            grad = other_ref[pl.ds((block - 2) * rows, rows), :].astype(jnp.float32)
        hat = hat_ref[here, :]
        live_grad = g_ref[here, :].astype(jnp.float32)
        grad_resid = live_grad + norm_back(grad, params_ref[4:5, :], hat, inv_ref[here, 0:1])
        resid_bf[here, :] = bf(grad_resid)
        if block == 0:
            resid_ref[...] = grad_resid
            sums_ref[2:3, :] = jnp.sum(grad * hat, axis=0, keepdims=True)
            sums_ref[3:4, :] = jnp.sum(grad, axis=0, keepdims=True)
            sums_ref[4:5, :] = jnp.sum(grad_resid, axis=0, keepdims=True)
            sums_ref[5:6, :] = jnp.sum(live_grad, axis=0, keepdims=True)
    sums_ref[6:7, :] = fc_sums_ref[0:1, :]
    sums_ref[7:8, :] = jnp.zeros((1, width), jnp.float32)
    grad_mixed[...] = bf(dot(resid_bf[...], w_ref[:, three:], 1, 0))
    for head in range(heads):
        at_q = slice(head * HD, (head + 1) * HD)
        at_k = slice(quarter + head * HD, quarter + (head + 1) * HD)
        at_v = slice(2 * quarter + head * HD, 2 * quarter + (head + 1) * HD)
        sum_q = jnp.zeros((1, HD), jnp.float32)
        sum_v = jnp.zeros((1, HD), jnp.float32)
        for index in range(2):
            part = pl.ds(index * group, group)
            prob = prob_ref[index * heads + head]
            mixed_grad = grad_mixed[part, at_q]
            grad_prob = dot(mixed_grad, qkv_ref[part, at_v], 1, 1)
            delta = jnp.sum(prob * grad_prob, axis=-1, keepdims=True)
            grad_scores = bf(prob * (grad_prob - delta) * SCALE)
            grad_query = dot(grad_scores, qkv_ref[part, at_k], 1, 0)
            grad_key = dot(grad_scores, qkv_ref[part, at_q], 0, 0)
            grad_value = dot(bf(prob), mixed_grad, 0, 0)
            sum_q += jnp.sum(grad_query, axis=0, keepdims=True)
            sum_v += jnp.sum(grad_value, axis=0, keepdims=True)
            joined_ref[part, at_q] = bf(grad_query)
            joined_ref[part, at_k] = bf(grad_key)
            joined_ref[part, at_v] = bf(grad_value)
        sums_ref[7:8, at_q] = sum_q
        sums_ref[7:8, at_k] = sum_v
    whole = dot(joined_ref[...], w_ref[:, :three], 1, 1)
    with_hat = jnp.zeros((1, width), jnp.float32)
    plain = jnp.zeros((1, width), jnp.float32)
    for block in range(4):
        part = whole[block * rows : (block + 1) * rows]
        with_hat += jnp.sum(part * one_ref[pl.ds(block * rows, rows), :], axis=0, keepdims=True)
        plain += jnp.sum(part, axis=0, keepdims=True)
    keep_ref[...] = whole[:group]
    send_ref[...] = bf(whole[group:])
    sums_ref[0:1, :] = with_hat
    sums_ref[1:2, :] = plain
    parts = (
        bf(dot(normed_ref[...], joined_ref[...], 0, 0)),
        bf(dot(resid_bf[...], mixed_ref[...], 0, 0)),
    )
    count = width // chips
    half = count // 2
    shared = d_one_ref.shape[0] // chips - count
    if shared:
        sums = sums_ref[...]
        sums = bf(jnp.concatenate([sums, jnp.zeros_like(sums)], axis=0))
    for chip in range(chips):
        start = chip * (count + shared)
        for part, at in zip(parts, (slice(0, three), slice(three, width))):
            d_one_ref[start : start + half, at] = part[chip * count : chip * count + half]
            d_one_ref[start + half + shared : start + count + shared, at] = part[
                chip * count + half : (chip + 1) * count
            ]
        if shared:
            d_one_ref[start + half : start + half + shared, :] = sums
    if shared:
        send_far(table_ref, d_one_ref, ahead_ref, back_ref)


def back(table, h2_own, h2_other, fc_sums, params, saved, chips, shared):
    all_rows, width = saved[0].shape
    f32, b16 = jnp.float32, jnp.bfloat16
    quarter = width // 4
    outs = (
        ((width + chips * shared, width), b16),
        ((all_rows // 2, width), f32),
        ((all_rows // 2, width), b16),
        ((all_rows // 4, width), f32),
        ((8, width), f32),
        ((width // chips // 2 + shared, width), b16),
        ((width // chips // 2, width), b16),
    )
    ins = (h2_own, h2_other, fc_sums, params, *saved)
    return pl.pallas_call(
        functools.partial(back_kernel, chips=chips),
        out_shape=[jax.ShapeDtypeStruct(*one) for one in outs],
        in_specs=[SMEM] + [VMEM] * len(ins),
        out_specs=[VMEM] * len(outs),
        scratch_shapes=[
            pltpu.VMEM((all_rows, 3 * quarter), b16),
            pltpu.VMEM((all_rows, width), b16),
            pltpu.VMEM((all_rows, quarter), b16),
        ],
        compiler_params=pltpu.CompilerParams(vmem_limit_bytes=VMEM_LIMIT),
        cost_estimate=pl.CostEstimate(flops=2 << 30, bytes_accessed=10 << 20, transcendentals=0),
    )(table, *ins)


def weights_two_kernel(table_ref, normed_ref, grad_ref, g_ref, act_ref, out_ref, *far_refs):
    hidden = act_ref.shape[1]
    out_ref[:, :hidden] = bf(dot(normed_ref[...], grad_ref[...], 0, 0))
    out_ref[:, hidden:] = bf(dot(g_ref[...], act_ref[...], 0, 0))
    if far_refs:
        send_far(table_ref, out_ref, *far_refs)


def weights_two(table, normed, grad, grad_all, act, far_rows):
    ins = (normed, grad, grad_all, act)
    b16 = jnp.bfloat16
    out = jax.ShapeDtypeStruct((normed.shape[1], 2 * act.shape[1]), b16)
    far = jax.ShapeDtypeStruct((far_rows, 2 * act.shape[1]), b16)
    outs = (out, far, far) if far_rows else (out,)
    return pl.pallas_call(
        weights_two_kernel,
        out_shape=outs,
        in_specs=[SMEM] + [VMEM] * len(ins),
        out_specs=[VMEM] * len(outs),
        compiler_params=pltpu.CompilerParams(vmem_limit_bytes=VMEM_LIMIT),
        cost_estimate=pl.CostEstimate(flops=1 << 30, bytes_accessed=4 << 20, transcendentals=0),
    )(table, *ins)


def mlp_out_kernel(act_ref, w_ref, keep_ref, send_ref):
    half = keep_ref.shape[0]
    part = dot(act_ref[...], w_ref[...], 1, 1)
    keep_ref[...] = part[:half]
    send_ref[...] = bf(part[half:])


def mlp_out(act, w_out):
    rows, width = act.shape[0] // 2, w_out.shape[0]
    return pl.pallas_call(
        mlp_out_kernel,
        out_shape=(
            jax.ShapeDtypeStruct((rows, width), jnp.float32),
            jax.ShapeDtypeStruct((rows, width), jnp.bfloat16),
        ),
        in_specs=[VMEM] * 2,
        out_specs=[VMEM] * 2,
        compiler_params=pltpu.CompilerParams(vmem_limit_bytes=8 << 20),
        cost_estimate=pl.CostEstimate(flops=1 << 29, bytes_accessed=3 << 20, transcendentals=0),
    )(act, w_out)


def inputs_kernel(x_ref, keep_ref, met_ref, resid_ref, params_ref, out_ref):
    hat, inv = normalize(x_ref[...].astype(jnp.float32))
    grad = keep_ref[...] + met_ref[...].astype(jnp.float32)
    out_ref[...] = bf(resid_ref[...] + norm_back(grad, params_ref[0:1, :], hat, inv))


def grad_inputs(tokens, kept, met, resid, params):
    ins = (tokens, kept, met, resid, params)
    return pl.pallas_call(
        inputs_kernel,
        out_shape=jax.ShapeDtypeStruct(tokens.shape, jnp.bfloat16),
        in_specs=[VMEM] * len(ins),
        out_specs=VMEM,
        compiler_params=pltpu.CompilerParams(vmem_limit_bytes=8 << 20),
        cost_estimate=pl.CostEstimate(flops=0, bytes_accessed=1 << 20, transcendentals=0),
    )(*ins)


def pair_kernel(keep_ref, met_ref, own_ref, send_ref):
    rows = own_ref.shape[0]
    pair = keep_ref[...] + met_ref[...].astype(jnp.float32)
    own_ref[...] = pair[:rows]
    send_ref[...] = bf(pair[rows:])


def block(
    tokens,
    segment_ids,
    valid_counts,
    ln1_gain,
    ln1_bias,
    w_qkv,
    b_qv,
    w_proj,
    b_proj,
    ln2_gain,
    ln2_bias,
    w_fc,
    b_fc,
    w_out,
    b_out,
    grad_out,
):
    me = lax.axis_index("dp")
    core = me % 2
    _, width = tokens.shape
    shard_rows = w_fc.shape[0]
    quarter = w_qkv.shape[2] // 2

    def chip_rows(kept, sent):
        return jnp.concatenate([kept, core_swap(sent)], axis=0)

    ring = use_ring(shard_rows)
    chips = lax.axis_size("dp") // 2
    rows_out = jax.ShapeDtypeStruct(tokens.shape, jnp.bfloat16)
    pair_out = jax.ShapeDtypeStruct((2,) + tokens.shape, jnp.bfloat16)
    (own_pair,) = ring_call(own_pair_kernel, (pair_out,), valid_counts, tokens, grad_out)
    vectors = (ln1_gain, ln1_bias, b_qv, b_proj, ln2_gain, ln2_bias, b_fc, b_out)
    table, params = setting(vectors, quarter, chips if ring else 0)
    if ring:
        keep_one, send_one, keep_two, send_two = pack(w_qkv, w_proj, w_fc, w_out)
        one_pieces = gather_rows(chip_rows(keep_one, send_one))
        two_pieces = gather_rows(chip_rows(keep_two, send_two))
        blocks = 2 * chips
    else:
        blocks = 1
        full_four = [
            core_part(lax.all_gather(shard, "dp", axis=0, tiled=True), core, 1)
            for shard in (w_qkv[0], w_qkv[1], w_qkv[2], w_proj, w_fc, w_out)
        ]
        one_pieces = [jnp.concatenate(full_four[:4], axis=1)]
        two_pieces = [jnp.concatenate(full_four[4:], axis=1)]
    x_pair = x_swap(own_pair)
    core_pair = core_swap(own_pair)
    far_pair = core_swap(x_pair)
    x_all, grad_all = join((own_pair, x_pair, core_pair, far_pair))
    segs = jnp.stack([segment_ids, core_swap(segment_ids)])

    one_full, proj_own = assemble_one(table, one_pieces, width, blocks)
    proj_x = x_swap(proj_own)
    mixed = attention(table, one_full, x_all, segs, params, False)[0]
    proj_c, proj_cx = core_swap(proj_own), core_swap(proj_x)
    mixed_x = x_swap(mixed)
    mixed_c, mixed_cx = core_swap(mixed), core_swap(mixed_x)
    (
        resid_own_one, hat_two, inv_two, normed_two, act_bf, grad_pre_bf, h2_keep, h2_send, fc_sums,
        out_full,
    ) = mlp(
        table,
        two_pieces,
        (mixed, mixed_x, mixed_c, mixed_cx),
        (proj_own, proj_x, proj_c, proj_cx),
        x_all,
        grad_all,
        params,
        blocks,
    )
    h2_pair = h2_keep + core_swap(h2_send).astype(jnp.float32)
    h2_own = h2_pair + swap_halves(x_swap(bf(h2_pair))).astype(jnp.float32)
    h2_other = core_swap(bf(h2_own))
    d_two_terms, *far = weights_two(
        table, normed_two, grad_pre_bf, grad_all, act_bf, shard_rows if ring else 0
    )
    if ring:
        kept, other, _ = reduce_ring(table, d_two_terms, far, shard_rows)
        d_fc, d_out = finish_two(table, kept, other)
    else:
        kept, other = reduce_plain(d_two_terms)
        d_fc, d_out = (
            jnp.concatenate(
                [jnp.where(core == 0, mine, theirs), jnp.where(core == 0, theirs, mine)], axis=1
            )
            for mine, theirs in zip(jnp.split(kept, 2, axis=1), jnp.split(other, 2, axis=1))
        )
    mlp_keep, mlp_send = mlp_out(act_bf, out_full)
    mlp_own, mlp_met = rows_to_owners(mlp_keep, mlp_send)
    (block_out,) = ring_call(
        block_out_kernel, (rows_out,), valid_counts, resid_own_one, mlp_own, mlp_met, params
    )

    shared = 16 if ring else 0
    normed_one, hat_one, qkv, prob, mixed_own = attention(
        table, one_full, x_all, segs, params, True
    )
    saved = (grad_all, hat_two, inv_two, one_full, qkv, prob, normed_one, hat_one, mixed_own)
    d_one_terms, h1_keep, h1_send, resid_own, sums, *far = back(
        table, h2_own, h2_other, fc_sums, params, saved, chips if ring else 1, shared
    )
    if ring:
        kept, other, own_sums = reduce_ring(table, d_one_terms, far, shard_rows)
        x_sums = x_swap(own_sums[0])
        d_qkv, d_proj, sums, d_bfc, d_qv = finish_one(table, kept, other, shard_rows)
        sums = sums + (x_sums + core_swap(x_sums))
    else:
        reach = 2
        while reach < lax.axis_size("dp"):
            pairs_now = [(i, i ^ reach) for i in range(lax.axis_size("dp"))]
            sums = sums + lax.ppermute(sums, "dp", pairs_now)
            reach *= 2
        sums = jnp.where(jnp.arange(8)[:, None] < 6, sums + x_swap(sums), sums)
        met = core_swap(sums)
        low, high = jnp.where(core == 0, sums, met), jnp.where(core == 0, met, sums)
        sums = sums + met
        d_bfc = jnp.concatenate([low[6], high[6]])
        d_qv = jnp.concatenate(
            [rows[7, : 2 * quarter].reshape(2, quarter) for rows in (low, high)], axis=1
        )
        kept, other = reduce_plain(d_one_terms)
        low, high = jnp.where(core == 0, kept, other), jnp.where(core == 0, other, kept)
        d_four = jnp.concatenate(
            [rows.reshape(shard_rows, 4, quarter) for rows in (low, high)], axis=2
        ).transpose(1, 0, 2)
        d_qkv, d_proj = d_four[:3], d_four[3]
    h1_own, h1_met = rows_to_owners(h1_keep, h1_send)
    grad_input = grad_inputs(tokens, h1_own, h1_met, resid_own, params)
    return (
        block_out,
        grad_input,
        sums[0],
        sums[1],
        d_qkv,
        d_qv,
        d_proj,
        sums[4],
        sums[2],
        sums[3],
        d_fc,
        d_bfc,
        d_out,
        sums[5],
    )


def solution(mesh):
    return jax.shard_map(
        block,
        mesh=mesh,
        in_specs=(
            P(("dp", "tensor"), None),
            P("dp"),
            P("dp"),
            P(),
            P(),
            P(None, "dp", "tensor"),
            P(None, "tensor"),
            P("dp", "tensor"),
            P(),
            P(),
            P(),
            P("dp", "tensor"),
            P("tensor"),
            P("dp", "tensor"),
            P(),
            P(("dp", "tensor"), None),
        ),
        out_specs=(
            P(("dp", "tensor"), None),
            P(("dp", "tensor"), None),
            P(),
            P(),
            P(None, "dp", "tensor"),
            P(None, "tensor"),
            P("dp", "tensor"),
            P(),
            P(),
            P(),
            P("dp", "tensor"),
            P("tensor"),
            P("dp", "tensor"),
            P(),
        ),
        check_vma=False,
    )
```
